32 devices in a mesh: gx: 2 (over x), gy: 16 (over z, y, core).
Axes of the slice: x: 2, y: 2, z: 4, core: 2. Of those that a mesh axis runs over, the one named last changes fastest.
Arguments:
- hidden_in: bfloat16 [32, 512, 768], P(('gx', 'gy')), may hold values from -6 to 6
- segment_ids: int32 [32, 512], P(('gx', 'gy')), may hold values from 0 to 511, as said below
- positions: int32 [32, 512], P(('gx', 'gy')), may hold values from 0 to 511, as said below
- token_mask: int32 [32, 512], P(('gx', 'gy')), may hold values from 0 to 1, as said below
- cotangent: bfloat16 [32, 512, 768], P(('gx', 'gy')), may hold values from -6 to 6
- qkv_weight: bfloat16 [442368], P(('gx', 'gy')), may hold values from -0.4375 to 0.4375
- out_weight: bfloat16 [589824], P(('gx', 'gy')), may hold values from -1.75 to 1.75
- up_weight: bfloat16 [589824], P(('gx', 'gy')), may hold values from -0.4375 to 0.4375
- down_weight: bfloat16 [589824], P(('gx', 'gy')), may hold values from -0.21875 to 0.21875
- biases: bfloat16 [7680], P(('gx', 'gy')), may hold values from -2.5 to 2.5
- gains: bfloat16 [1536], P(('gx', 'gy')), may hold values from 0.25 to 1.75
Outputs:
- layer_output: bfloat16 [32, 512, 768], P(('gx', 'gy'))
- input_grad: float32 [32, 512, 768], P(('gx', 'gy'))
- qkv_weight_grad: float32 [442368], P(('gx', 'gy'))
- out_weight_grad: float32 [589824], P(('gx', 'gy'))
- up_weight_grad: float32 [589824], P(('gx', 'gy'))
- down_weight_grad: float32 [589824], P(('gx', 'gy'))
- biases_grad: float32 [7680], P(('gx', 'gy'))
- gains_grad: float32 [1536], P(('gx', 'gy'))
The draws below stay inside these ranges and needn't reach their ends.
Inputs may be any that keep to these rules, and one draw needn't show every extreme that they name: `segment_ids`: within a row segment ids start at 0 and never fall; a document is a run of tokens with one id. `positions`: positions count from 0 at the first token of each document. `token_mask`: padding stands only at the end of a row, at most 128 tokens.
All inputs are finite; a program needn't handle non-finite values.
Results may differ from the reference program's by a relative error of at most 0.012.
Values may be sent and summed in bfloat16 or wider, within the bound.
A program may use at most 128 MiB of HBM per device.

```python
import jax
import jax.numpy as jnp
from jax import lax

D = 768
FF = 3072
HEADS = 12
GROUPS = 4
L = 512
BATCH = 32


def layout(key):
    base = jax.random.fold_in(key, 11)
    flag_key, pad_key = jax.random.split(base)
    places = jnp.arange(L, dtype=jnp.int32)
    row_index = jnp.arange(BATCH, dtype=jnp.int32)[:, None]
    random_starts = (jax.random.randint(flag_key, (BATCH, L), 0, max(L // 4, 2)) == 0) | (places == 0)[None, :]
    starts_here = jnp.where(row_index == 0, (places == 0)[None, :], random_starts)
    starts_here = jnp.where(row_index == 1, True, starts_here)
    segment = jnp.cumsum(starts_here.astype(jnp.int32), axis=1) - 1
    first_place = lax.cummax(jnp.where(starts_here, places[None, :], 0), axis=1)
    pad_count = jax.random.randint(pad_key, (BATCH, 1), 0, L // 4 + 1)
    valid = (places[None, :] < L - pad_count).astype(jnp.int32)
    return (segment.astype(jnp.int32), (places[None, :] - first_place).astype(jnp.int32), valid)


def draw_segment_ids(key, part):
    return layout(key)[0]


def draw_positions(key, part):
    return layout(key)[1]


def draw_token_mask(key, part):
    return layout(key)[2]


def levels(rng, dims, shards, low, top_value):
    level = 1.0
    for position, shards_of in shards:
        steps = jax.random.uniform(jax.random.fold_in(jax.random.fold_in(rng, 6), position), (shards_of,), jnp.float32, low / len(shards), top_value / len(shards))
        level = level * jnp.repeat(jnp.exp(steps), dims[position] // shards_of).reshape((-1,) + (1,) * (len(dims) - 1 - position))
    return level


def gaussian(rng, extent, width, limit, cuts=(), held_as=jnp.bfloat16):
    values = width * jax.random.normal(rng, extent, jnp.float32)
    if cuts:
        values = values * levels(rng, extent, cuts, -0.22, 0.18)
    return jnp.clip(values, -limit, limit).astype(held_as)


def setup_inputs(seed: int = 0) -> dict:
    seeds = jax.random.split(jax.random.key(seed), 12)
    return {
        "hidden_in": gaussian(seeds[0], (BATCH, L, D), 1.0, 6.0, ((0, 32),)),
        "segment_ids": draw_segment_ids(jax.random.fold_in(seeds[11], 71), 0),
        "positions": draw_positions(jax.random.fold_in(seeds[11], 71), 0),
        "token_mask": draw_token_mask(jax.random.fold_in(seeds[11], 71), 0),
        "cotangent": gaussian(seeds[4], (BATCH, L, D), 1.0, 6.0, ((0, 32),)),
        "qkv_weight": gaussian(seeds[5], (3 * D * D // 4,), (D // GROUPS) ** -0.5, 0.4375, ((0, 32),)),
        "out_weight": gaussian(seeds[6], (D * D,), (D // 64) ** -0.5, 1.75, ((0, 32),)),
        "up_weight": gaussian(seeds[7], (D * FF // 4,), (D // GROUPS) ** -0.5, 0.4375, ((0, 32),)),
        "down_weight": gaussian(seeds[8], (FF * D // 4,), (FF // GROUPS) ** -0.5, 0.21875, ((0, 32),)),
        "biases": gaussian(seeds[9], (6 * D + FF,), 0.3, 2.5, ((0, 32),)),
        "gains": jnp.clip(1.0 + 0.15 * jax.random.normal(seeds[10], (2 * D,), jnp.float32), 0.25, 1.75).astype(jnp.bfloat16),
    }


epsilon = 1e-05
highest = lax.Precision.HIGHEST

@jax.custom_vjp
def low(v):
    return lax.optimization_barrier(v.astype(jnp.bfloat16)).astype(jnp.float32)

@jax.custom_vjp
def low_back(v):
    return v

def low_keep(v):
    return (low(v), None)

def low_pass(kept, grad):
    return (grad,)

def back_keep(v):
    return (v, None)

def back_low(kept, grad):
    return (low(grad),)
low.defvjp(low_keep, low_pass)
low_back.defvjp(back_keep, back_low)

def layer_norm(summed, gain_row, shift_row):
    centred = summed - lax.optimization_barrier(jnp.mean(summed, axis=-1, keepdims=True))
    variance = lax.optimization_barrier(jnp.mean(centred * centred, axis=-1, keepdims=True))
    return centred * lax.rsqrt(variance + epsilon) * gain_row + shift_row

def grouped(inputs, weight):
    groups, width_in, width_out = weight.shape
    shaped = inputs.reshape(inputs.shape[:-1] + (groups, width_in))
    result = jnp.einsum('rlgi,gio->rlgo', shaped, weight, precision=highest)
    return result

def allowed_keys(seg_rows, pos_rows, valid_rows):
    places = jnp.arange(seg_rows.shape[-1], dtype=jnp.int32)
    starts = places[None, :] - pos_rows
    same_doc = (seg_rows[:, :, None] == seg_rows[:, None, :]) & (starts[:, :, None] == starts[:, None, :])
    open_key = (valid_rows[:, None, :] == 1) | (places[:, None] == places[None, :])[None]
    return same_doc & open_key

def block_rows(params, rows_in, seg_rows, pos_rows, valid_rows):
    qkv_flat, out_flat, up_flat, down_flat, bias_vector, gain_vector = params
    row_count, length, model_width = rows_in.shape
    group_width = model_width // GROUPS
    qkv_matrix = qkv_flat.reshape(GROUPS, group_width, 3 * group_width)
    out_matrix = out_flat.reshape(model_width, model_width)
    up_matrix = up_flat.reshape(GROUPS, group_width, FF // GROUPS)
    down_matrix = down_flat.reshape(GROUPS, FF // GROUPS, group_width)
    flat_shape = (row_count, length, model_width)
    head_shape = (row_count, length, HEADS, model_width // HEADS)
    projected = grouped(rows_in, qkv_matrix)
    queries = low(low_back(projected[..., :group_width].reshape(flat_shape) + bias_vector[:model_width]))
    key_rows = low(low_back(projected[..., group_width:2 * group_width].reshape(flat_shape)))
    value_rows = low(low_back(projected[..., 2 * group_width:].reshape(flat_shape) + bias_vector[model_width:2 * model_width]))
    scores = low_back(jnp.einsum('rqhd,rkhd->rhqk', queries.reshape(head_shape), key_rows.reshape(head_shape), precision=highest) * 0.125)
    scores = jnp.where(allowed_keys(seg_rows, pos_rows, valid_rows)[:, None], scores, -1000000000.0)
    probability = low(jax.nn.softmax(scores, axis=-1))
    context = jnp.einsum('rhqk,rkhd->rqhd', probability, value_rows.reshape(head_shape), precision=highest).reshape(flat_shape)
    context = low(low_back(context))
    attended = low_back(jnp.einsum('rli,io->rlo', context, out_matrix, precision=highest) + bias_vector[2 * model_width:3 * model_width])
    first_out = layer_norm(rows_in + attended, gain_vector[:model_width], bias_vector[3 * model_width:4 * model_width])
    hidden_pre = low_back(grouped(low(first_out), up_matrix).reshape(row_count, length, FF) + bias_vector[4 * model_width:4 * model_width + FF])
    active = low(jax.nn.gelu(hidden_pre, approximate=False))
    branch_out = low_back(grouped(active, down_matrix).reshape(flat_shape) + bias_vector[4 * model_width + FF:5 * model_width + FF])
    return layer_norm(first_out + branch_out, gain_vector[model_width:], bias_vector[5 * model_width + FF:])

def reference(hidden_in, segment_ids, positions, token_mask, cotangent, qkv_weight, out_weight, up_weight, down_weight, biases, gains):
    per_step = 8
    step_count = BATCH // per_step

    def regroup(stacked):
        return stacked.reshape((step_count, per_step) + stacked.shape[1:])
    params = (qkv_weight.astype(jnp.float32), out_weight.astype(jnp.float32), up_weight.astype(jnp.float32), down_weight.astype(jnp.float32), biases.astype(jnp.float32), gains.astype(jnp.float32))
    inputs = regroup(hidden_in.astype(jnp.float32))
    seg_groups = regroup(segment_ids.astype(jnp.int32))
    pos_groups = regroup(positions.astype(jnp.int32))
    valid_groups = regroup(token_mask.astype(jnp.int32))

    def forward(params, inputs):

        def one_step(packed):
            rows_in, seg_rows, pos_rows, valid_rows = packed
            return jax.checkpoint(block_rows)(params, rows_in, seg_rows, pos_rows, valid_rows)
        return lax.map(one_step, (inputs, seg_groups, pos_groups, valid_groups))
    output, pullback = jax.vjp(forward, params, inputs)
    param_grads, input_grad = pullback(regroup(cotangent.astype(jnp.float32)))
    return (output.reshape(BATCH, L, D).astype(jnp.bfloat16), input_grad.reshape(BATCH, L, D), param_grads[0], param_grads[1], param_grads[2], param_grads[3], param_grads[4], param_grads[5])
```

```python
import jax
import jax.numpy as jnp
from jax import lax
from jax.experimental import pallas as pl
from jax.experimental.pallas import tpu as pltpu
from jax.sharding import PartitionSpec as P

FF = 3072
HEADS = 12
GROUPS = 4
epsilon = 1e-05
f32 = jnp.float32
bf16 = jnp.bfloat16


def dot(a, b):
    return lax.dot_general(a, b, (((1,), (0,)), ((), ())), preferred_element_type=f32)

def dot_nt(a, b):
    return lax.dot_general(a, b, (((1,), (1,)), ((), ())), preferred_element_type=f32)

def dot_tn(a, b):
    return lax.dot_general(a, b, (((0,), (0,)), ((), ())), preferred_element_type=f32)

def fold(v):
    return jnp.sum(v.reshape(v.shape[0] // 8, 8, v.shape[1]), axis=0)


def stage_qkv(s):
    T, D = s.x.shape
    gw = D // GROUPS
    for pair in range(2):
        parts = []
        for g in (2 * pair, 2 * pair + 1):
            parts.append(dot(s.x[:, g * gw:(g + 1) * gw], s.wqkv[g]))
        cols = pl.ds(pair * 2 * gw, 2 * gw)
        def both(i):
            return jnp.concatenate([parts[0][:, i * gw:(i + 1) * gw], parts[1][:, i * gw:(i + 1) * gw]], axis=1)
        s.q[:, cols] = (both(0) + s.bias(0, pair * 2 * gw, 2 * gw)).astype(bf16) * jnp.asarray(0.125, bf16)
        s.k[:, cols] = both(1).astype(bf16)
        s.v[:, cols] = (both(2) + s.bias(D, pair * 2 * gw, 2 * gw)).astype(bf16)


def stage_mask(s):
    T, D = s.x.shape
    place = lax.broadcasted_iota(jnp.int32, (1, T), 1)
    code = s.seg[...] * 1024 + (place - s.pos[...])
    keyed = jnp.where(s.tok[...] == 1, code, -1)
    keyed = jnp.broadcast_to(keyed.astype(f32), (128, T)).T
    code_f = code.astype(f32)
    for c in range(T // 128):
        cols = pl.ds(c * 128, 128)
        same = keyed == code_f[:, c * 128:(c + 1) * 128]
        rows = lax.broadcasted_iota(jnp.int32, (T, 128), 0)
        lanes = lax.broadcasted_iota(jnp.int32, (T, 128), 1) + c * 128
        s.mask[:, cols] = jnp.where(same | (rows == lanes), 0.0, -1000000000.0)


def stage_attn_fwd(s, lo, hi):
    T, D = s.x.shape
    lane = lax.broadcasted_iota(jnp.int32, (1, 128), 1)
    def pair_step(pr, carry):
        cols = pl.ds(pl.multiple_of(pr * 128, 128), 128)
        q2 = s.q[:, cols]
        k2 = s.k[:, cols]
        vT = s.v[:, cols].T
        outs = []
        for h in range(2):
            keep = (lane < 64) if h == 0 else (lane >= 64)
            qm = jnp.where(keep, q2, jnp.zeros_like(q2))
            sT = dot_nt(k2, qm) + s.mask[...]
            m = jnp.max(sT, axis=0, keepdims=True)
            e = jnp.exp(sT - m)
            l = jnp.sum(e, axis=0, keepdims=True)
            p = (e * (1.0 / l)).astype(bf16)
            s.pT[2 * pr + h] = p
            outs.append(dot(vT[64 * h:64 * h + 64], p))
        cT = jnp.concatenate(outs, axis=0).astype(bf16)
        s.ctxT[pl.ds(pl.multiple_of(pr * 128, 128), 128), :] = cT
        s.ctx[:, cols] = cT.T
        return carry
    lax.fori_loop(lo, hi, pair_step, 0)


def stage_ln1(s):
    T, D = s.x.shape
    s.att[...] = dot(s.ctx[...], s.wout[...])
    R = 32
    def step(i, carry):
        rows = pl.ds(pl.multiple_of(i * R, R), R)
        u = s.x[rows, :].astype(f32) + (s.att[rows, :] + s.bias(2 * D, 0, D))
        c = u - jnp.sum(u, axis=1, keepdims=True) * (1.0 / D)
        r = lax.rsqrt(jnp.sum(c * c, axis=1, keepdims=True) * (1.0 / D) + epsilon)
        n = c * r
        s.n1[rows, :] = n
        s.r1[rows, :] = jnp.broadcast_to(r, (R, 128))
        s.first_low[rows, :] = (n * s.gain(0) + s.bias(3 * D, 0, D)).astype(bf16)
        return carry
    lax.fori_loop(0, T // R, step, 0)


def gelu_parts(z):
    phi = 0.5 * (1.0 + lax.erf(z * 0.7071067811865476))
    dens = jnp.exp(z * z * -0.5) * 0.3989422804014327
    return z * phi, phi + z * dens


def stage_ffn(s):
    T, D = s.x.shape
    gw, fg = D // GROUPS, FF // GROUPS
    R = 128
    def step(i, carry):
        rows = pl.ds(pl.multiple_of(i * R, R), R)
        for pair in range(2):
            outs = []
            for g in (2 * pair, 2 * pair + 1):
                z = dot(s.first_low[rows, g * gw:(g + 1) * gw], s.wup[g]) + s.bias(4 * D, g * fg, fg)
                act, gp = gelu_parts(z)
                act = act.astype(bf16)
                s.active[rows, g * fg:(g + 1) * fg] = act
                s.gp[rows, g * fg:(g + 1) * fg] = gp
                outs.append(dot(act, s.wdown[g]))
            s.att[rows, pair * 2 * gw:(pair + 1) * 2 * gw] = jnp.concatenate(outs, axis=1)
        return carry
    lax.fori_loop(0, T // R, step, 0)


def stage_ln2(s):
    T, D = s.x.shape
    R = 32
    for a in (s.acc_g2, s.acc_s2, s.acc_down):
        a[...] = jnp.zeros_like(a)
    def step(i, carry):
        rows = pl.ds(pl.multiple_of(i * R, R), R)
        first = s.n1[rows, :] * s.gain(0) + s.bias(3 * D, 0, D)
        u = first + (s.att[rows, :] + s.bias(4 * D + FF, 0, D))
        c = u - jnp.sum(u, axis=1, keepdims=True) * (1.0 / D)
        r = lax.rsqrt(jnp.sum(c * c, axis=1, keepdims=True) * (1.0 / D) + epsilon)
        n = c * r
        s.out[rows, :] = (n * s.gain(D) + s.bias(5 * D + FF, 0, D)).astype(bf16)
        dy = s.cot[rows, :].astype(f32)
        s.acc_g2[...] += fold(dy * n)
        s.acc_s2[...] += fold(dy)
        e = dy * s.gain(D)
        m1 = jnp.sum(e, axis=1, keepdims=True) * (1.0 / D)
        m2 = jnp.sum(e * n, axis=1, keepdims=True) * (1.0 / D)
        du = r * (e - m1 - n * m2)
        s.dsec[rows, :] = du
        dl = du.astype(bf16)
        s.douter[rows, :] = dl
        s.acc_down[...] += fold(dl.astype(f32))
        return carry
    lax.fori_loop(0, T // R, step, 0)


def stage_ffn_back(s):
    T, D = s.x.shape
    gw, fg = D // GROUPS, FF // GROUPS
    R = 128
    s.acc_up[...] = jnp.zeros_like(s.acc_up)
    def step(i, carry):
        rows = pl.ds(pl.multiple_of(i * R, R), R)
        for pair in range(2):
            outs = []
            for g in (2 * pair, 2 * pair + 1):
                da = dot_nt(s.douter[rows, g * gw:(g + 1) * gw], s.wdown[g])
                di = (da * s.gp[rows, g * fg:(g + 1) * fg]).astype(bf16)
                s.dinner[rows, g * fg:(g + 1) * fg] = di
                s.acc_up[:, g * fg:(g + 1) * fg] += fold(di.astype(f32))
                outs.append(dot_nt(di, s.wup[g]))
            s.att[rows, pair * 2 * gw:(pair + 1) * 2 * gw] = jnp.concatenate(outs, axis=1)
        return carry
    lax.fori_loop(0, T // R, step, 0)


def stage_down_grad(s, put):
    T, D = s.x.shape
    gw, fg = D // GROUPS, FF // GROUPS
    for g in range(GROUPS):
        put(g, dot_tn(s.active[:, g * fg:(g + 1) * fg], s.douter[:, g * gw:(g + 1) * gw]))


def stage_up_grad(s, put):
    T, D = s.x.shape
    gw, fg = D // GROUPS, FF // GROUPS
    for g in range(GROUPS):
        put(g, dot_tn(s.first_low[:, g * gw:(g + 1) * gw], s.dinner[:, g * fg:(g + 1) * fg]))


def stage_ln1_back(s):
    T, D = s.x.shape
    R = 32
    for a in (s.acc_g1, s.acc_s1, s.acc_out):
        a[...] = jnp.zeros_like(a)
    def step(i, carry):
        rows = pl.ds(pl.multiple_of(i * R, R), R)
        dy = s.dsec[rows, :] + s.att[rows, :]
        n = s.n1[rows, :]
        s.acc_g1[...] += fold(dy * n)
        s.acc_s1[...] += fold(dy)
        e = dy * s.gain(0)
        m1 = jnp.sum(e, axis=1, keepdims=True) * (1.0 / D)
        m2 = jnp.sum(e * n, axis=1, keepdims=True) * (1.0 / D)
        du = s.r1[rows, 0:1] * (e - m1 - n * m2)
        s.dsec[rows, :] = du
        dl = du.astype(bf16)
        s.dattn[rows, :] = dl
        s.acc_out[...] += fold(dl.astype(f32))
        return carry
    lax.fori_loop(0, T // R, step, 0)


def stage_out_grad(s, put):
    put(dot(s.ctxT[...], s.dattn[...]))
    s.dctx[...] = dot_nt(s.dattn[...], s.wout[...]).astype(bf16)


def stage_attn_back(s, lo, hi):
    T, D = s.x.shape
    lane = lax.broadcasted_iota(jnp.int32, (1, 128), 1)
    def pair_step(pr, carry):
        start = pl.multiple_of(pr * 128, 128)
        cols = pl.ds(start, 128)
        q2 = s.q[:, cols]
        v2 = s.v[:, cols]
        dc2 = s.dctx[:, cols]
        kT = s.k[:, cols].T
        prod = (s.ctxT[cols, :].astype(f32)) * (dc2.T.astype(f32))
        dk, dv, dqT = [], [], []
        for h in range(2):
            keep = (lane < 64) if h == 0 else (lane >= 64)
            qm = jnp.where(keep, q2, jnp.zeros_like(q2))
            dcm = jnp.where(keep, dc2, jnp.zeros_like(dc2))
            p = s.pT[2 * pr + h]
            delta = jnp.sum(prod[64 * h:64 * h + 64], axis=0, keepdims=True)
            dp = dot_nt(v2, dcm)
            ds = (p.astype(f32) * (dp - delta)).astype(bf16)
            dv.append(dot(p, dcm))
            dk.append(dot(ds, qm))
            dqT.append(dot(kT[64 * h:64 * h + 64], ds))
        s.dv[:, cols] = (dv[0] + dv[1]).astype(bf16)
        s.dk[:, cols] = (dk[0] + dk[1]).astype(bf16)
        s.dq[:, cols] = (jnp.concatenate(dqT, axis=0) * 0.125).astype(bf16).T
        return carry
    lax.fori_loop(lo, hi, pair_step, 0)


def stage_qkv_grad(s, put):
    T, D = s.x.shape
    gw = D // GROUPS
    for pair in range(2):
        outs = []
        for g in (2 * pair, 2 * pair + 1):
            c = slice(g * gw, (g + 1) * gw)
            joined = jnp.concatenate([s.dq[:, c], s.dk[:, c], s.dv[:, c]], axis=1)
            put(g, dot_tn(s.x[:, c], joined))
            outs.append(dot_nt(joined, s.wqkv[g]))
        cols = slice(pair * 2 * gw, (pair + 1) * 2 * gw)
        s.din[:, cols] = s.dsec[:, cols] + jnp.concatenate(outs, axis=1)


MESH = pl.DeviceIdType.MESH
ARRAYS = ("small", "qkv", "out", "up", "down")


class Names:
    pass


class Torus:
    def __init__(self, sizes):
        self.nx, gy = sizes
        self.nc = 2 if gy % 2 == 0 else 1
        self.nz = 4 if (gy // self.nc) % 4 == 0 else 1
        self.ny = gy // self.nc // self.nz
        self.count = self.nx * gy
        self.planes = [(i, j) for i in range(self.nx) for j in range(self.ny) if i or j]
        self.planes.sort(key=lambda o: -((o[0] != 0) + (o[1] != 0)))

    def locate(self):
        gy = lax.axis_index("gy")
        self.x = lax.axis_index("gx")
        self.c = gy % self.nc
        self.y = gy // self.nc % self.ny
        self.z = gy // (self.nc * self.ny)

    def device(self, x, y, z, c):
        return (x, (z * self.ny + y) * self.nc + c)

    def place(self, x, y, z, c):
        return ((c * self.nx + x) * self.ny + y) * self.nz + z

    def place_of(self, index):
        gy_size = self.nz * self.ny * self.nc
        x, gy = index // gy_size, index % gy_size
        return self.place(x, gy // self.nc % self.ny, gy // (self.nc * self.ny), gy % self.nc)

    def plane(self, offset):
        return (self.x + offset[0]) % self.nx, (self.y + offset[1]) % self.ny

    def peers(self):
        found = [self.device(self.x, self.y, (self.z + d) % self.nz, self.c) for d in range(1, self.nz)]
        for o in self.planes:
            px, py = self.plane(o)
            found.append(self.device(px, py, self.z, self.c))
        if self.nc > 1:
            found.append(self.device(self.x, self.y, self.z, 1 - self.c))
        return found


def remote(src, dst, send, recv, device):
    return pltpu.make_async_remote_copy(
        src_ref=src, dst_ref=dst, send_sem=send, recv_sem=recv, device_id=device, device_id_type=MESH
    )


class Gather:
    def __init__(self, t, own, buf, sems):
        self.t, self.own, self.buf = t, own, buf
        self.local, self.s1, self.r1, self.s2, self.r2, self.s3, self.r3 = sems

    def first_copies(self):
        t = self.t
        mine = t.place(t.x, t.y, t.z, t.c)
        return [
            remote(self.own, self.buf.at[mine], self.s1.at[d], self.r1.at[d],
                   t.device(t.x, t.y, (t.z + d) % t.nz, t.c))
            for d in range(1, t.nz)
        ]

    def local_copy(self):
        t = self.t
        return pltpu.make_async_copy(self.own, self.buf.at[t.place(t.x, t.y, t.z, t.c)], self.local.at[0])

    def second_copies(self):
        t = self.t
        part = self.buf.at[pl.ds(t.place(t.x, t.y, 0, t.c), t.nz)]
        found = []
        for k, o in enumerate(t.planes):
            px, py = t.plane(o)
            found.append(remote(part, part, self.s2.at[k], self.r2.at[k], t.device(px, py, t.z, t.c)))
        return found

    def third_copy(self, k, offset):
        t = self.t
        px, py = (t.x + t.nx - offset[0]) % t.nx, (t.y + t.ny - offset[1]) % t.ny
        part = self.buf.at[pl.ds(t.place(px, py, 0, t.c), t.nz)]
        return remote(part, part, self.s3.at[k], self.r3.at[k], t.device(t.x, t.y, t.z, 1 - t.c))

    def begin(self):
        self.local_copy().start()
        for c in self.first_copies():
            c.start()

    def spread(self):
        for c in self.first_copies():
            c.wait_recv()
        self.local_copy().wait()
        for c in self.second_copies():
            c.start()
        if self.t.nc > 1:
            self.third_copy(len(self.t.planes), (0, 0)).start()

    def share(self):
        for k, c in enumerate(self.second_copies()):
            c.wait_recv()
            if self.t.nc > 1:
                self.third_copy(k, self.t.planes[k]).start()

    def finish(self):
        t = self.t
        for c in self.first_copies() + self.second_copies():
            c.wait_send()
        if t.nc > 1:
            for k, o in enumerate(t.planes + [(0, 0)]):
                c = self.third_copy(k, o)
                c.wait_recv()
                c.wait_send()


class Scatter:
    def __init__(self, t, buf, ra, rb, rc, out, sems):
        self.t, self.buf, self.ra, self.rb, self.rc, self.out = t, buf, ra, rb, rc, out
        self.sc = ra.at[len(t.planes)]
        self.s1, self.r1, self.s2, self.r2, self.s3, self.r3 = sems

    def core_copy(self, k, offset):
        t = self.t
        px, py = t.plane(offset)
        part = self.buf.at[pl.ds(t.place(px, py, 0, 1 - t.c), t.nz)]
        return remote(part, self.ra.at[k], self.s1.at[k], self.r1.at[k], t.device(t.x, t.y, t.z, 1 - t.c))

    def plane_copy(self, k, offset):
        t = self.t
        px, py = t.plane(offset)
        return remote(self.ra.at[k], self.rb.at[k], self.s2.at[k], self.r2.at[k], t.device(px, py, t.z, t.c))

    def line_copy(self, d):
        t = self.t
        to = (t.z + d) % t.nz
        return remote(self.sc.at[to], self.rc.at[d], self.s3.at[d], self.r3.at[d], t.device(t.x, t.y, to, t.c))

    def begin(self):
        if self.t.nc > 1:
            for k, o in enumerate(self.t.planes + [(0, 0)]):
                self.core_copy(k, o).start()

    def chip_sum(self, k, offset):
        t = self.t
        px, py = t.plane(offset)
        part = self.buf[pl.ds(t.place(px, py, 0, t.c), t.nz)].astype(f32)
        if t.nc > 1:
            self.core_copy(k, offset).wait_recv()
            part = part + self.ra[k].astype(f32)
        return part

    def planes(self):
        for k, o in enumerate(self.t.planes):
            self.ra[k] = self.chip_sum(k, o).astype(self.ra.dtype)
            self.plane_copy(k, o).start()

    def line(self):
        t = self.t
        total = self.chip_sum(len(t.planes), (0, 0))
        for k, o in enumerate(t.planes):
            self.plane_copy(k, o).wait_recv()
            total = total + self.rb[k].astype(f32)
        self.sc[...] = total.astype(self.sc.dtype)
        for d in range(1, t.nz):
            self.line_copy(d).start()

    def finish(self):
        t = self.t
        total = self.sc[t.z].astype(f32)
        for d in range(1, t.nz):
            self.line_copy(d).wait_recv()
            total = total + self.rc[d].astype(f32)
        self.out[...] = total
        for d in range(1, t.nz):
            self.line_copy(d).wait_send()
        for k, o in enumerate(t.planes):
            self.plane_copy(k, o).wait_send()
        if t.nc > 1:
            for k, o in enumerate(t.planes + [(0, 0)]):
                self.core_copy(k, o).wait_send()


def joined_rows(t, buf, first, many):
    return jnp.concatenate([buf[t.place_of(first + j)].astype(f32) for j in range(many)], axis=0).astype(bf16)


def assemble(s, t, name):
    buf = s.held[name]
    if name == "small":
        nb, ng = s.small_sizes
        for d in range(t.count):
            p = t.place_of(d)
            s.bias_v[0:1, nb * d:nb * d + nb] = buf[p, 0:1, 0:nb]
            s.gain_v[0:1, ng * d:ng * d + ng] = buf[p, 1:2, 0:ng]
        return
    per = t.count // GROUPS
    for g in range(GROUPS):
        value = joined_rows(t, buf, g * per, per)
        if name == "qkv":
            s.wqkv[g] = value
        elif name == "out":
            gw = s.wout.shape[0] // GROUPS
            s.wout[g * gw:(g + 1) * gw, :] = value
        elif name == "up":
            s.wup[g] = value
        else:
            s.wdown[g] = value


def lay_out(s, t, name, g, value):
    per = t.count // GROUPS
    buf = s.held[name]
    rows = value.shape[0] // per
    for j in range(per):
        buf[t.place_of(g * per + j)] = value[rows * j:rows * j + rows].astype(bf16)


def lay_out_small(s, t):
    T, D = s.x.shape
    nb, ng = s.small_sizes
    def rs(v):
        return jnp.sum(v, axis=0, keepdims=True)
    s.bias_v[:, 0:D] = rs(s.dq[...].astype(f32))
    s.bias_v[:, D:2 * D] = rs(s.dv[...].astype(f32))
    s.bias_v[:, 2 * D:3 * D] = rs(s.acc_out[...])
    s.bias_v[:, 3 * D:4 * D] = rs(s.acc_s1[...])
    s.bias_v[:, 4 * D:4 * D + FF] = rs(s.acc_up[...])
    s.bias_v[:, 4 * D + FF:5 * D + FF] = rs(s.acc_down[...])
    s.bias_v[:, 5 * D + FF:] = rs(s.acc_s2[...])
    s.gain_v[:, 0:D] = rs(s.acc_g1[...])
    s.gain_v[:, D:] = rs(s.acc_g2[...])
    buf = s.held["small"]
    for d in range(t.count):
        p = t.place_of(d)
        buf[p, 0:1, 0:nb] = s.bias_v[0:1, nb * d:nb * d + nb]
        buf[p, 1:2, 0:ng] = s.gain_v[0:1, ng * d:ng * d + ng]


def layer_kernel(names, t, small_sizes, *refs):
    s = Names()
    for n, r in zip(names, refs, strict=True):
        setattr(s, n, r)
    D = s.x.shape[1]
    s.small_sizes = small_sizes
    s.bias = lambda base, off, w: s.bias_v[0:1, base + off:base + off + w]
    s.gain = lambda base: s.gain_v[0:1, base:base + D]
    s.held = {n: getattr(s, "held_" + n) for n in ARRAYS}
    t.locate()

    barrier = pltpu.get_barrier_semaphore()
    peers = t.peers()
    for peer in peers:
        pl.semaphore_signal(barrier, inc=1, device_id=peer, device_id_type=MESH)
    pl.semaphore_wait(barrier, len(peers))

    gather, scatter = {}, {}
    for i, n in enumerate(ARRAYS):
        gather[n] = Gather(t, getattr(s, "in_" + n), s.held[n],
                           [getattr(s, "g_" + k).at[i] for k in ("local", "s1", "r1", "s2", "r2", "s3", "r3")])
        scatter[n] = Scatter(t, s.held[n], *[getattr(s, k + "_" + n) for k in ("ra", "rb", "rc", "grad")],
                             [getattr(s, "h_" + k).at[i] for k in ("s1", "r1", "s2", "r2", "s3", "r3")])

    gather["small"].begin()
    gather["qkv"].begin()
    stage_mask(s)
    gather["small"].spread()
    gather["qkv"].spread()
    gather["out"].begin()
    gather["small"].share()
    gather["qkv"].share()
    gather["out"].spread()
    gather["up"].begin()
    gather["small"].finish()
    gather["qkv"].finish()
    assemble(s, t, "small")
    assemble(s, t, "qkv")
    stage_qkv(s)
    gather["up"].spread()
    gather["down"].begin()
    gather["out"].share()
    stage_attn_fwd(s, 0, 2)
    gather["down"].spread()
    stage_attn_fwd(s, 2, 4)
    gather["up"].share()
    stage_attn_fwd(s, 4, 6)
    gather["down"].share()
    gather["out"].finish()
    assemble(s, t, "out")
    stage_ln1(s)
    gather["up"].finish()
    gather["down"].finish()
    assemble(s, t, "up")
    assemble(s, t, "down")
    stage_ffn(s)
    stage_ln2(s)
    stage_down_grad(s, lambda g, v: lay_out(s, t, "down", g, v))
    scatter["down"].begin()
    stage_ffn_back(s)
    scatter["down"].planes()
    stage_up_grad(s, lambda g, v: lay_out(s, t, "up", g, v))
    scatter["up"].begin()
    stage_ln1_back(s)
    def put_out(v):
        gw = D // GROUPS
        for g in range(GROUPS):
            lay_out(s, t, "out", g, v[g * gw:(g + 1) * gw])
    scatter["up"].planes()
    stage_out_grad(s, put_out)
    scatter["out"].begin()
    stage_attn_back(s, 0, 2)
    scatter["out"].planes()
    scatter["down"].line()
    stage_attn_back(s, 2, 4)
    scatter["up"].line()
    scatter["down"].finish()
    stage_attn_back(s, 4, 6)
    scatter["out"].line()
    scatter["up"].finish()
    stage_qkv_grad(s, lambda g, v: lay_out(s, t, "qkv", g, v))
    scatter["qkv"].begin()
    lay_out_small(s, t)
    scatter["small"].begin()
    scatter["qkv"].planes()
    scatter["small"].planes()
    scatter["out"].finish()
    scatter["qkv"].line()
    scatter["small"].line()
    scatter["qkv"].finish()
    scatter["small"].finish()


def body(sizes, hidden_in, segment_ids, positions, token_mask, cotangent, qkv_weight, out_weight, up_weight, down_weight, biases, gains):
    rows, T, D = hidden_in.shape
    assert rows == 1
    gw = D // GROUPS
    t = Torus(sizes)
    nb, ng = biases.shape[0], gains.shape[0]
    depth = D // t.count
    blocks = {
        "small": ((8, 256), f32),
        "qkv": ((depth, 3 * gw), bf16),
        "out": ((depth, D), bf16),
        "up": ((depth, FF // GROUPS), bf16),
        "down": ((FF // t.count, gw), bf16),
    }
    small = jnp.concatenate([
        jnp.pad(biases.astype(f32), (0, 256 - nb))[None],
        jnp.pad(gains.astype(f32), (0, 256 - ng))[None],
        jnp.zeros((6, 256), f32),
    ], axis=0)
    inputs = {
        "x": hidden_in[0], "seg": segment_ids, "pos": positions, "tok": token_mask, "cot": cotangent[0],
        "in_small": small,
        "in_qkv": qkv_weight.reshape(blocks["qkv"][0]),
        "in_out": out_weight.reshape(blocks["out"][0]),
        "in_up": up_weight.reshape(blocks["up"][0]),
        "in_down": down_weight.reshape(blocks["down"][0]),
    }
    outputs = {"out": ((T, D), bf16), "din": ((T, D), f32)}
    for n in ARRAYS:
        outputs["grad_" + n] = (blocks[n][0], f32)
    scratch = dict(
        mask=((T, T), f32), q=((T, D), bf16), k=((T, D), bf16), v=((T, D), bf16), pT=((HEADS, T, T), bf16),
        ctx=((T, D), bf16), ctxT=((D, T), bf16), att=((T, D), f32), n1=((T, D), f32), r1=((T, 128), f32),
        first_low=((T, D), bf16), active=((T, FF), bf16), gp=((T, FF), f32), dsec=((T, D), f32),
        douter=((T, D), bf16), dinner=((T, FF), bf16), dattn=((T, D), bf16), dctx=((T, D), bf16),
        dq=((T, D), bf16), dk=((T, D), bf16), dv=((T, D), bf16),
        acc_g2=((8, D), f32), acc_s2=((8, D), f32), acc_down=((8, D), f32), acc_up=((8, FF), f32),
        acc_g1=((8, D), f32), acc_s1=((8, D), f32), acc_out=((8, D), f32),
        bias_v=((1, nb * t.count), f32), gain_v=((1, ng * t.count), f32),
        wqkv=((GROUPS, gw, 3 * gw), bf16), wout=((D, D), bf16),
        wup=((GROUPS, gw, FF // GROUPS), bf16), wdown=((GROUPS, FF // GROUPS, gw), bf16),
    )
    np_ = len(t.planes)
    for n in ARRAYS:
        shape, kind = blocks[n]
        scratch["held_" + n] = ((t.count,) + shape, kind)
        scratch["ra_" + n] = ((np_ + 1, t.nz) + shape, kind)
        scratch["rb_" + n] = ((np_, t.nz) + shape, kind)
        scratch["rc_" + n] = ((t.nz,) + shape, kind)
    shapes = [pltpu.VMEM(*scratch[n]) for n in scratch]
    sems = dict(g_local=1, g_s1=t.nz, g_r1=t.nz, g_s2=np_, g_r2=np_, g_s3=np_ + 1, g_r3=np_ + 1,
                h_s1=np_ + 1, h_r1=np_ + 1, h_s2=np_, h_r2=np_, h_s3=t.nz, h_r3=t.nz)
    shapes += [pltpu.SemaphoreType.DMA((len(ARRAYS), sems[n])) for n in sems]
    names = list(inputs) + list(outputs) + list(scratch) + list(sems)
    vm = pl.BlockSpec(memory_space=pltpu.VMEM)
    found = pl.pallas_call(
        lambda *refs: layer_kernel(names, t, (nb, ng), *refs),
        out_shape=[jax.ShapeDtypeStruct(*outputs[n]) for n in outputs],
        in_specs=[vm] * len(inputs),
        out_specs=[vm] * len(outputs),
        scratch_shapes=shapes,
        compiler_params=pltpu.CompilerParams(
            collective_id=0, has_side_effects=True, vmem_limit_bytes=67043328
        ),
        name="layer",
    )(*inputs.values())
    o = dict(zip(outputs, found))
    return (
        o["out"][None], o["din"][None], o["grad_qkv"].reshape(-1), o["grad_out"].reshape(-1), o["grad_up"].reshape(-1),
        o["grad_down"].reshape(-1), o["grad_small"][0, :nb], o["grad_small"][1, :ng],
    )


def solution(mesh):
    whole = P(("gx", "gy"))
    rows2 = P(("gx", "gy"), None)
    rows3 = P(("gx", "gy"), None, None)
    sizes = (mesh.shape["gx"], mesh.shape["gy"])
    return jax.shard_map(
        lambda *args: body(sizes, *args),
        mesh=mesh,
        in_specs=(rows3, rows2, rows2, rows2, rows3) + (whole,) * 6,
        out_specs=(rows3, rows3) + (whole,) * 6,
        check_vma=False,
    )
```

```python
import jax
import jax.numpy as jnp
from jax import lax
from jax.experimental import pallas as pl
from jax.experimental.pallas import tpu as pltpu
from jax.sharding import PartitionSpec as P

FF = 3072
HEADS = 12
GROUPS = 4
epsilon = 1e-05
f32 = jnp.float32
bf16 = jnp.bfloat16


def dot(a, b):
    return lax.dot_general(a, b, (((1,), (0,)), ((), ())), preferred_element_type=f32)

def dot_nt(a, b):
    return lax.dot_general(a, b, (((1,), (1,)), ((), ())), preferred_element_type=f32)

def dot_tn(a, b):
    return lax.dot_general(a, b, (((0,), (0,)), ((), ())), preferred_element_type=f32)

def fold(v):
    return jnp.sum(v.reshape(v.shape[0] // 8, 8, v.shape[1]), axis=0)


def stage_qkv(s, half):
    T, D = s.x.shape
    gw = D // GROUPS
    cols = pl.ds(pl.multiple_of(half * 2 * gw, 128), 2 * gw)
    value_cols = pl.ds(pl.multiple_of(half * 2 * gw + D, 128), 2 * gw)
    xh = s.x[:, cols]
    parts = [dot(xh[:, i * gw:(i + 1) * gw], s.wqkv[2 * half + i]) for i in range(2)]
    def both(i):
        return jnp.concatenate([parts[0][:, i * gw:(i + 1) * gw], parts[1][:, i * gw:(i + 1) * gw]], axis=1)
    s.q[:, cols] = (both(0) + s.bias_v[0:1, cols]).astype(bf16) * jnp.asarray(0.125, bf16)
    s.k[:, cols] = both(1).astype(bf16)
    s.v[:, cols] = (both(2) + s.bias_v[0:1, value_cols]).astype(bf16)


def stage_mask(s):
    T, D = s.x.shape
    place = lax.broadcasted_iota(jnp.int32, (1, T), 1)
    code = s.seg[...] * 1024 + (place - s.pos[...])
    keyed = jnp.where(s.tok[...] == 1, code, -1)
    keyed = jnp.broadcast_to(keyed.astype(f32), (128, T)).T
    code_f = code.astype(f32)
    for c in range(T // 128):
        cols = pl.ds(c * 128, 128)
        same = keyed == code_f[:, c * 128:(c + 1) * 128]
        rows = lax.broadcasted_iota(jnp.int32, (T, 128), 0)
        lanes = lax.broadcasted_iota(jnp.int32, (T, 128), 1) + c * 128
        s.mask[:, cols] = jnp.where(same | (rows == lanes), 0.0, -1000000000.0)


def stage_attn_fwd(s, lo, hi):
    T, D = s.x.shape
    lane = lax.broadcasted_iota(jnp.int32, (1, 128), 1)
    def pair_step(pr, carry):
        cols = pl.ds(pl.multiple_of(pr * 128, 128), 128)
        q2 = s.q[:, cols]
        k2 = s.k[:, cols]
        vT = s.v[:, cols].T
        outs = []
        for h in range(2):
            keep = (lane < 64) if h == 0 else (lane >= 64)
            qm = jnp.where(keep, q2, jnp.zeros_like(q2))
            sT = dot_nt(k2, qm) + s.mask[...]
            m = jnp.max(sT, axis=0, keepdims=True)
            e = jnp.exp(sT - m)
            l = jnp.sum(e, axis=0, keepdims=True)
            p = (e * (1.0 / l)).astype(bf16)
            s.pT[2 * pr + h] = p
            outs.append(dot(vT[64 * h:64 * h + 64], p))
        cT = jnp.concatenate(outs, axis=0).astype(bf16)
        s.ctxT[pl.ds(pl.multiple_of(pr * 128, 128), 128), :] = cT
        s.ctx[:, cols] = cT.T
        return carry
    lax.fori_loop(lo, hi, pair_step, 0)


def stage_ln1(s):
    T, D = s.x.shape
    s.att[...] = dot(s.ctx[...], s.wout[...])
    R = 32
    def step(i, carry):
        rows = pl.ds(pl.multiple_of(i * R, R), R)
        u = s.x[rows, :].astype(f32) + (s.att[rows, :] + s.bias(2 * D, 0, D))
        c = u - jnp.sum(u, axis=1, keepdims=True) * (1.0 / D)
        r = lax.rsqrt(jnp.sum(c * c, axis=1, keepdims=True) * (1.0 / D) + epsilon)
        n = c * r
        s.n1[rows, :] = n
        s.r1[rows, :] = jnp.broadcast_to(r, (R, 128))
        s.first_low[rows, :] = (n * s.gain(0) + s.bias(3 * D, 0, D)).astype(bf16)
        return carry
    lax.fori_loop(0, T // R, step, 0)


def gelu_parts(z):
    phi = 0.5 * (1.0 + lax.erf(z * 0.7071067811865476))
    dens = jnp.exp(z * z * -0.5) * 0.3989422804014327
    return z * phi, phi + z * dens


def stage_ffn(s):
    T, D = s.x.shape
    gw, fg = D // GROUPS, FF // GROUPS
    R = 128
    def step(i, carry):
        rows = pl.ds(pl.multiple_of(i * R, R), R)
        for pair in range(2):
            outs = []
            for g in (2 * pair, 2 * pair + 1):
                z = dot(s.first_low[rows, g * gw:(g + 1) * gw], s.wup[g]) + s.bias(4 * D, g * fg, fg)
                act, gp = gelu_parts(z)
                act = act.astype(bf16)
                s.active[rows, g * fg:(g + 1) * fg] = act
                s.gp[rows, g * fg:(g + 1) * fg] = gp
                outs.append(dot(act, s.wdown[g]))
            s.att[rows, pair * 2 * gw:(pair + 1) * 2 * gw] = jnp.concatenate(outs, axis=1)
        return carry
    lax.fori_loop(0, T // R, step, 0)


def stage_ln2(s):
    T, D = s.x.shape
    R = 32
    for a in (s.acc_g2, s.acc_s2, s.acc_down):
        a[...] = jnp.zeros_like(a)
    def step(i, carry):
        rows = pl.ds(pl.multiple_of(i * R, R), R)
        first = s.n1[rows, :] * s.gain(0) + s.bias(3 * D, 0, D)
        u = first + (s.att[rows, :] + s.bias(4 * D + FF, 0, D))
        c = u - jnp.sum(u, axis=1, keepdims=True) * (1.0 / D)
        r = lax.rsqrt(jnp.sum(c * c, axis=1, keepdims=True) * (1.0 / D) + epsilon)
        n = c * r
        s.out[rows, :] = (n * s.gain(D) + s.bias(5 * D + FF, 0, D)).astype(bf16)
        dy = s.cot[rows, :].astype(f32)
        s.acc_g2[...] += fold(dy * n)
        s.acc_s2[...] += fold(dy)
        e = dy * s.gain(D)
        m1 = jnp.sum(e, axis=1, keepdims=True) * (1.0 / D)
        m2 = jnp.sum(e * n, axis=1, keepdims=True) * (1.0 / D)
        du = r * (e - m1 - n * m2)
        s.dsec[rows, :] = du
        dl = du.astype(bf16)
        s.douter[rows, :] = dl
        s.acc_down[...] += fold(dl.astype(f32))
        return carry
    lax.fori_loop(0, T // R, step, 0)


def stage_ffn_back(s, lo, hi):
    T, D = s.x.shape
    gw, fg = D // GROUPS, FF // GROUPS
    R = 128
    if lo == 0:
        s.acc_up[...] = jnp.zeros_like(s.acc_up)
    def step(i, carry):
        rows = pl.ds(pl.multiple_of(i * R, R), R)
        for pair in range(2):
            outs = []
            for g in (2 * pair, 2 * pair + 1):
                da = dot_nt(s.douter[rows, g * gw:(g + 1) * gw], s.wdown[g])
                di = (da * s.gp[rows, g * fg:(g + 1) * fg]).astype(bf16)
                s.dinner[rows, g * fg:(g + 1) * fg] = di
                s.acc_up[:, g * fg:(g + 1) * fg] += fold(di.astype(f32))
                outs.append(dot_nt(di, s.wup[g]))
            s.att[rows, pair * 2 * gw:(pair + 1) * 2 * gw] = jnp.concatenate(outs, axis=1)
        return carry
    lax.fori_loop(T // R * lo // 4, T // R * hi // 4, step, 0)


def stage_down_grad(s, put):
    T, D = s.x.shape
    gw, fg = D // GROUPS, FF // GROUPS
    for g in range(GROUPS):
        put(g, dot_tn(s.active[:, g * fg:(g + 1) * fg], s.douter[:, g * gw:(g + 1) * gw]))


def stage_up_grad(s, put):
    T, D = s.x.shape
    gw, fg = D // GROUPS, FF // GROUPS
    for g in range(GROUPS):
        put(g, dot_tn(s.first_low[:, g * gw:(g + 1) * gw], s.dinner[:, g * fg:(g + 1) * fg]))


def stage_ln1_back(s):
    T, D = s.x.shape
    R = 32
    for a in (s.acc_g1, s.acc_s1, s.acc_out):
        a[...] = jnp.zeros_like(a)
    def step(i, carry):
        rows = pl.ds(pl.multiple_of(i * R, R), R)
        dy = s.dsec[rows, :] + s.att[rows, :]
        n = s.n1[rows, :]
        s.acc_g1[...] += fold(dy * n)
        s.acc_s1[...] += fold(dy)
        e = dy * s.gain(0)
        m1 = jnp.sum(e, axis=1, keepdims=True) * (1.0 / D)
        m2 = jnp.sum(e * n, axis=1, keepdims=True) * (1.0 / D)
        du = s.r1[rows, 0:1] * (e - m1 - n * m2)
        s.dsec[rows, :] = du
        dl = du.astype(bf16)
        s.dattn[rows, :] = dl
        s.acc_out[...] += fold(dl.astype(f32))
        return carry
    lax.fori_loop(0, T // R, step, 0)


def stage_out_grad(s, put):
    put(dot(s.ctxT[...], s.dattn[...]))
    s.dctx[...] = dot_nt(s.dattn[...], s.wout[...]).astype(bf16)


def stage_attn_back(s, lo, hi):
    T, D = s.x.shape
    lane = lax.broadcasted_iota(jnp.int32, (1, 128), 1)
    def pair_step(pr, carry):
        start = pl.multiple_of(pr * 128, 128)
        cols = pl.ds(start, 128)
        q2 = s.q[:, cols]
        v2 = s.v[:, cols]
        dc2 = s.dctx[:, cols]
        kT = s.k[:, cols].T
        prod = (s.ctxT[cols, :].astype(f32)) * (dc2.T.astype(f32))
        dk, dv, dqT = [], [], []
        for h in range(2):
            keep = (lane < 64) if h == 0 else (lane >= 64)
            qm = jnp.where(keep, q2, jnp.zeros_like(q2))
            dcm = jnp.where(keep, dc2, jnp.zeros_like(dc2))
            p = s.pT[2 * pr + h]
            delta = jnp.sum(prod[64 * h:64 * h + 64], axis=0, keepdims=True)
            dp = dot_nt(v2, dcm)
            ds = (p.astype(f32) * (dp - delta)).astype(bf16)
            dv.append(dot(p, dcm))
            dk.append(dot(ds, qm))
            dqT.append(dot(kT[64 * h:64 * h + 64], ds))
        s.dv[:, cols] = (dv[0] + dv[1]).astype(bf16)
        s.dk[:, cols] = (dk[0] + dk[1]).astype(bf16)
        s.dq[:, cols] = (jnp.concatenate(dqT, axis=0) * 0.125).astype(bf16).T
        return carry
    lax.fori_loop(lo, hi, pair_step, 0)


def stage_qkv_grad(s, half, put):
    T, D = s.x.shape
    gw = D // GROUPS
    cols = pl.ds(pl.multiple_of(half * 2 * gw, 128), 2 * gw)
    xh, dq, dk, dv = s.x[:, cols], s.dq[:, cols], s.dk[:, cols], s.dv[:, cols]
    for i in range(2):
        c = slice(i * gw, (i + 1) * gw)
        joined = jnp.concatenate([dq[:, c], dk[:, c], dv[:, c]], axis=1)
        s.joined[2 * half + i] = joined
        put(2 * half + i, i, dot_tn(xh[:, c], joined))


def stage_input_grad(s):
    T, D = s.x.shape
    gw = D // GROUPS
    for pair in range(2):
        cols = slice(pair * 2 * gw, (pair + 1) * 2 * gw)
        outs = [dot_nt(s.joined[g], s.wqkv[g]) for g in (2 * pair, 2 * pair + 1)]
        s.din[:, cols] = s.dsec[:, cols] + jnp.concatenate(outs, axis=1)


MESH = pl.DeviceIdType.MESH
ARRAYS = ("small", "qkv", "out", "up", "down")
NEAR = ("small", "qkv")


class Names:
    pass


class Torus:
    def __init__(self, sizes):
        self.nx, gy = sizes
        self.nc = 2
        assert gy % self.nc == 0
        self.nz = 4 if (gy // self.nc) % 4 == 0 else 1
        self.ny = gy // self.nc // self.nz
        self.count = self.nx * gy
        self.square = self.nx == 2 and self.ny == 2
        self.flat = self.ny * self.nz

    def locate(self):
        gy = lax.axis_index("gy")
        self.x = lax.axis_index("gx")
        self.c = gy % self.nc
        self.y = gy // self.nc % self.ny
        self.z = gy // (self.nc * self.ny)

    def device(self, x, y, z, c):
        return (x, (z * self.ny + y) * self.nc + c)

    def sibling(self):
        return self.device(self.x, self.y, self.z, 1 - self.c)

    def place(self, x, y, z, c):
        return ((c * self.nx + x) * self.ny + y) * self.nz + z

    def place_in(self, x, gy):
        return self.place(x, gy // self.nc % self.ny, gy // (self.nc * self.ny), gy % self.nc)

    def place_of(self, index):
        gy_size = self.flat * self.nc
        return self.place_in(index // gy_size, index % gy_size)

    def shift(self, o):
        return (self.x + o[0]) % self.nx, (self.y + o[1]) % self.ny

    def turn(self, o):
        return (self.y + o[0]) % self.ny, (self.z + o[1]) % self.nz

    def plane_offsets(self):
        return [(i, j) for i in range(self.nx) for j in range(self.ny) if i or j]

    def flat_offsets(self):
        return [(i, j) for j in range(self.nz) for i in range(self.ny) if i or j]

    def peers(self):
        found = [self.device(self.x, y, z, self.c) for y, z in (self.turn(o) for o in self.flat_offsets())]
        for o in self.plane_offsets():
            if o[0] == 0 or (self.square and o == (1, 1)):
                continue
            px, py = self.shift(o)
            found.append(self.device(px, py, self.z, self.c))
        return found + [self.sibling()]


def remote(src, dst, send, recv, device):
    return pltpu.make_async_remote_copy(
        src_ref=src, dst_ref=dst, send_sem=send, recv_sem=recv, device_id=device, device_id_type=MESH
    )


class NearGather:
    def __init__(self, t, own, buf, sems):
        self.t, self.own, self.buf = t, own, buf
        self.local, self.s1, self.r1, self.s2, self.r2, self.s3, self.r3 = sems

    def chunk(self, x, c):
        return self.buf.at[pl.ds(self.t.place(x, 0, 0, c), self.t.flat)]

    def local_copy(self):
        t = self.t
        return pltpu.make_async_copy(self.own, self.buf.at[t.place(t.x, t.y, t.z, t.c)], self.local.at[0])

    def near_copies(self):
        t = self.t
        mine = self.buf.at[t.place(t.x, t.y, t.z, t.c)]
        found = []
        for k, o in enumerate(t.flat_offsets()):
            py, pz = t.turn(o)
            found.append(remote(self.own, mine, self.s1.at[k], self.r1.at[k], t.device(t.x, py, pz, t.c)))
        return found

    def far_copy(self, d):
        t = self.t
        part = self.chunk(t.x, t.c)
        return remote(part, part, self.s2.at[d], self.r2.at[d], t.device((t.x + d) % t.nx, t.y, t.z, t.c))

    def core_copy(self, d):
        t = self.t
        part = self.chunk((t.x + t.nx - d) % t.nx, t.c)
        return remote(part, part, self.s3.at[d], self.r3.at[d], t.sibling())

    def begin(self):
        self.local_copy().start()
        for c in self.near_copies():
            c.start()

    def spread(self):
        for c in self.near_copies():
            c.wait_recv()
        self.local_copy().wait()
        self.core_copy(0).start()
        for d in range(1, self.t.nx):
            self.far_copy(d).start()

    def near_done(self):
        self.core_copy(0).wait_recv()

    def share(self):
        for d in range(1, self.t.nx):
            self.far_copy(d).wait_recv()
            self.core_copy(d).start()

    def far_done(self):
        for d in range(1, self.t.nx):
            self.core_copy(d).wait_recv()

    def close(self):
        for c in self.near_copies():
            c.wait_send()
        for d in range(self.t.nx):
            self.core_copy(d).wait_send()
            if d:
                self.far_copy(d).wait_send()


class NearScatter:
    def __init__(self, t, buf, ra, rb, rc, sems):
        self.t, self.buf, self.ra, self.rb, self.rc = t, buf, ra, rb, rc
        self.s1, self.r1, self.s2, self.r2, self.s3, self.r3 = sems

    def core_copy(self, d):
        t = self.t
        part = self.buf.at[pl.ds(t.place((t.x + d) % t.nx, 0, 0, 1 - t.c), t.flat)]
        return remote(part, self.ra.at[d], self.s1.at[d], self.r1.at[d], t.sibling())

    def far_copy(self, d):
        t = self.t
        return remote(self.ra.at[d], self.rb.at[d], self.s2.at[d], self.r2.at[d],
                      t.device((t.x + d) % t.nx, t.y, t.z, t.c))

    def flat_copy(self, k, o):
        t = self.t
        py, pz = t.turn(o)
        return remote(self.ra.at[0, py * t.nz + pz], self.rc.at[k], self.s3.at[k], self.r3.at[k],
                      t.device(t.x, py, pz, t.c))

    def chip_sum(self, d):
        t = self.t
        self.core_copy(d).wait_recv()
        part = self.buf[pl.ds(t.place((t.x + d) % t.nx, 0, 0, t.c), t.flat)]
        return part.astype(f32) + self.ra[d].astype(f32)

    def begin_far(self):
        for d in range(1, self.t.nx):
            self.core_copy(d).start()

    def far(self):
        for d in range(1, self.t.nx):
            self.ra[d] = self.chip_sum(d).astype(self.ra.dtype)
            self.far_copy(d).start()

    def begin_near(self):
        self.core_copy(0).start()

    def near(self):
        total = self.chip_sum(0)
        for d in range(1, self.t.nx):
            self.far_copy(d).wait_recv()
            total = total + self.rb[d].astype(f32)
        self.ra[0] = total.astype(self.ra.dtype)
        for k, o in enumerate(self.t.flat_offsets()):
            self.flat_copy(k, o).start()

    def total(self):
        t = self.t
        total = self.ra[0, t.y * t.nz + t.z].astype(f32)
        for k, o in enumerate(t.flat_offsets()):
            self.flat_copy(k, o).wait_recv()
            total = total + self.rc[k].astype(f32)
        return total

    def close(self):
        for k, o in enumerate(self.t.flat_offsets()):
            self.flat_copy(k, o).wait_send()
        for d in range(self.t.nx):
            self.core_copy(d).wait_send()
            if d:
                self.far_copy(d).wait_send()


class Planes:
    def route(self):
        t = self.t
        if t.square:
            self.offsets = [(t.c, 1 - t.c), (1 - t.c, t.c)]
        else:
            self.offsets = t.plane_offsets()

    def slot(self, o):
        return o[0] * self.t.ny + o[1]

    def to(self, o):
        px, py = self.t.shift(o)
        return self.t.device(px, py, self.t.z, self.t.c)


class Gather(Planes):
    def __init__(self, t, own, buf, sems):
        self.t, self.own, self.buf = t, own, buf
        self.local, self.s1, self.r1, self.s2, self.r2, self.s3, self.r3 = sems
        self.route()

    def chunk(self, x, y):
        return self.buf.at[pl.ds(self.t.place(x, y, 0, self.t.c), self.t.nz)]

    def local_copy(self):
        t = self.t
        return pltpu.make_async_copy(self.own, self.buf.at[t.place(t.x, t.y, t.z, t.c)], self.local.at[0])

    def line_copies(self):
        t = self.t
        mine = self.buf.at[t.place(t.x, t.y, t.z, t.c)]
        return [
            remote(self.own, mine, self.s1.at[d], self.r1.at[d], t.device(t.x, t.y, (t.z + d) % t.nz, t.c))
            for d in range(1, t.nz)
        ]

    def plane_copy(self, k):
        part = self.chunk(self.t.x, self.t.y)
        return remote(part, part, self.s2.at[k], self.r2.at[k], self.to(self.offsets[k]))

    def relay_copy(self):
        part = self.chunk(*self.t.shift(self.offsets[0]))
        return remote(part, part, self.s2.at[2], self.r2.at[2], self.to(self.offsets[1]))

    def core_copy(self, o):
        t = self.t
        part = self.chunk((t.x + t.nx - o[0]) % t.nx, (t.y + t.ny - o[1]) % t.ny)
        k = self.slot(o)
        return remote(part, part, self.s3.at[k], self.r3.at[k], t.sibling())

    def begin(self):
        self.local_copy().start()
        for c in self.line_copies():
            c.start()

    def spread(self):
        for c in self.line_copies():
            c.wait_recv()
        self.local_copy().wait()
        for k in range(len(self.offsets)):
            self.plane_copy(k).start()
        self.core_copy((0, 0)).start()

    def share(self):
        for k, o in enumerate(self.offsets):
            self.plane_copy(k).wait_recv()
            if self.t.square and k == 0:
                self.relay_copy().start()
            self.core_copy(o).start()

    def share_last(self):
        if self.t.square:
            self.relay_copy().wait_recv()
            self.core_copy((1, 1)).start()

    def done(self):
        for o in [(0, 0)] + self.t.plane_offsets():
            self.core_copy(o).wait_recv()

    def close(self):
        for c in self.line_copies():
            c.wait_send()
        for k in range(len(self.offsets)):
            self.plane_copy(k).wait_send()
        if self.t.square:
            self.relay_copy().wait_send()
        for o in [(0, 0)] + self.t.plane_offsets():
            self.core_copy(o).wait_send()


class Scatter(Planes):
    def __init__(self, t, buf, ra, rb, rc, sems):
        self.t, self.buf, self.ra, self.rb, self.rc = t, buf, ra, rb, rc
        self.s1, self.r1, self.s2, self.r2, self.s3, self.r3 = sems
        self.route()

    def core_copy(self, o):
        t = self.t
        px, py = t.shift(o)
        part = self.buf.at[pl.ds(t.place(px, py, 0, 1 - t.c), t.nz)]
        k = self.slot(o)
        return remote(part, self.ra.at[k], self.s1.at[k], self.r1.at[k], t.sibling())

    def plane_copy(self, k, o, to):
        return remote(self.ra.at[self.slot(o)], self.rb.at[k], self.s2.at[k], self.r2.at[k], self.to(to))

    def line_copy(self, d):
        t = self.t
        to = (t.z + d) % t.nz
        return remote(self.ra.at[0, to], self.rc.at[d], self.s3.at[d], self.r3.at[d], t.device(t.x, t.y, to, t.c))

    def hops(self):
        if self.t.square:
            a, b = self.offsets
            return [(0, (1, 1), b), (1, b, b), (2, a, a)]
        return [(k, o, o) for k, o in enumerate(self.offsets)]

    def chip_sum(self, o):
        t = self.t
        px, py = t.shift(o)
        part = self.buf[pl.ds(t.place(px, py, 0, t.c), t.nz)]
        return part.astype(f32) + self.ra[self.slot(o)].astype(f32)

    def begin(self):
        for o in self.t.plane_offsets() + [(0, 0)]:
            self.core_copy(o).start()

    def planes(self):
        for o in self.t.plane_offsets() + [(0, 0)]:
            self.core_copy(o).wait_recv()
        for k, o, to in self.hops()[:2] if self.t.square else self.hops():
            self.ra[self.slot(o)] = self.chip_sum(o).astype(self.ra.dtype)
            self.plane_copy(k, o, to).start()

    def planes_last(self):
        if self.t.square:
            hops = self.hops()
            self.plane_copy(*hops[0]).wait_recv()
            k, o, to = hops[2]
            self.ra[self.slot(o)] = (self.chip_sum(o) + self.rb[0].astype(f32)).astype(self.ra.dtype)
            self.plane_copy(k, o, to).start()

    def line(self):
        t = self.t
        total = self.chip_sum((0, 0))
        for k, o, to in self.hops()[1:] if t.square else self.hops():
            self.plane_copy(k, o, to).wait_recv()
            total = total + self.rb[k].astype(f32)
        self.ra[0] = total.astype(self.ra.dtype)
        for d in range(1, t.nz):
            self.line_copy(d).start()

    def total(self):
        t = self.t
        total = self.ra[0, t.z].astype(f32)
        for d in range(1, t.nz):
            self.line_copy(d).wait_recv()
            total = total + self.rc[d].astype(f32)
        return total

    def close(self):
        for d in range(1, self.t.nz):
            self.line_copy(d).wait_send()
        for hop in self.hops():
            self.plane_copy(*hop).wait_send()
        for o in self.t.plane_offsets() + [(0, 0)]:
            self.core_copy(o).wait_send()


def swap_halves(a, b):
    lane = lax.broadcasted_iota(jnp.int32, a.shape, 1)
    return jnp.where(lane < 64, pltpu.roll(a, 64, 1), pltpu.roll(b, 64, 1))


def lines_to_rows(lines, spare, rows, width):
    if width % 128 == 0:
        m = width // 128
        return jnp.concatenate([lines[pl.ds(j, rows, stride=m), :] for j in range(m)], axis=1).astype(bf16)
    m = width // 64
    q, half = m // 2, rows // 2
    a = [lines[pl.ds(j, half, stride=m), :] for j in range(m)]
    for j in range(q + 1):
        spare[j, pl.ds(0, half, stride=2), :] = a[j]
        spare[j, pl.ds(1, half, stride=2), :] = swap_halves(a[q + j], a[q + j + 1] if j < q else a[q + j])
    return jnp.concatenate([spare[j] for j in range(q)] + [spare[q][:, 0:64]], axis=1).astype(bf16)


def rows_to_lines(value, lines, spare):
    rows, width = value.shape
    if width % 128 == 0:
        m = width // 128
        for j in range(m):
            lines[pl.ds(j, rows, stride=m), :] = value[:, 128 * j:128 * j + 128]
        return
    m = width // 64
    q, half = m // 2, rows // 2
    for j in range(q):
        spare[j] = value[:, 128 * j:128 * j + 128]
    spare[q, :, 0:64] = value[:, 128 * q:width]
    even = [spare[j, pl.ds(0, half, stride=2), :] for j in range(q + 1)]
    odd = [spare[j, pl.ds(1, half, stride=2), :] for j in range(q + 1)]
    lane = lax.broadcasted_iota(jnp.int32, even[0].shape, 1)
    for j in range(q):
        lines[pl.ds(j, half, stride=m), :] = even[j]
        lines[pl.ds(q + 1 + j, half, stride=m), :] = swap_halves(odd[j], odd[j + 1])
    lines[pl.ds(q, half, stride=m), :] = jnp.where(lane < 64, even[q], pltpu.roll(odd[0], 64, 1))


def group_places(t, g, half, i):
    per = t.count // GROUPS
    if t.nx == 2:
        return [t.place_in(half, i * per + j) for j in range(per)]
    return [t.place_of(g * per + j) for j in range(per)]


def group_weight(s, t, name, places):
    buf = s.held[name]
    rows, width = s.group_shape[name]
    if s.lined:
        n = buf.shape[1]
        for j, p in enumerate(places):
            s.lines[n * j:n * j + n, :] = buf[p].astype(f32)
        return lines_to_rows(s.lines, s.spare[width], rows, width)
    return jnp.concatenate([buf[p].astype(f32) for p in places], axis=0).astype(bf16)


def assemble_small(s, t):
    nb, ng = s.small_sizes
    buf = s.held["small"]
    for d in range(t.count):
        p = t.place_of(d)
        s.bias_v[0:1, nb * d:nb * d + nb] = buf[p, 0:1, 0:nb]
        s.gain_v[0:1, ng * d:ng * d + ng] = buf[p, 0:1, nb:nb + ng]


def assemble_qkv(s, t, half):
    for i in range(2):
        g = 2 * half + i
        s.wqkv[g] = group_weight(s, t, "qkv", group_places(t, g, half, i))


def assemble(s, t, name):
    for g in range(GROUPS):
        value = group_weight(s, t, name, group_places(t, g, g // 2, g % 2))
        if name == "out":
            gw = s.wout.shape[0] // GROUPS
            s.wout[g * gw:(g + 1) * gw, :] = value
        elif name == "up":
            s.wup[g] = value
        else:
            s.wdown[g] = value


def lay_out(s, t, name, places, value):
    buf = s.held[name]
    if s.lined:
        n = buf.shape[1]
        rows_to_lines(value, s.lines, s.spare[value.shape[1]] if value.shape[1] % 128 else None)
        for j, p in enumerate(places):
            buf[p] = s.lines[n * j:n * j + n, :].astype(bf16)
        return
    rows = value.shape[0] // len(places)
    for j, p in enumerate(places):
        buf[p] = value[rows * j:rows * j + rows].astype(bf16)


def lay_out_small(s, t):
    T, D = s.x.shape
    nb, ng = s.small_sizes
    def rs(v):
        return jnp.sum(v, axis=0, keepdims=True)
    s.bias_v[:, 0:D] = rs(s.dq[...].astype(f32))
    s.bias_v[:, D:2 * D] = rs(s.dv[...].astype(f32))
    s.bias_v[:, 2 * D:3 * D] = rs(s.acc_out[...])
    s.bias_v[:, 3 * D:4 * D] = rs(s.acc_s1[...])
    s.bias_v[:, 4 * D:4 * D + FF] = rs(s.acc_up[...])
    s.bias_v[:, 4 * D + FF:5 * D + FF] = rs(s.acc_down[...])
    s.bias_v[:, 5 * D + FF:] = rs(s.acc_s2[...])
    s.gain_v[:, 0:D] = rs(s.acc_g1[...])
    s.gain_v[:, D:] = rs(s.acc_g2[...])
    buf = s.held["small"]
    for d in range(t.count):
        p = t.place_of(d)
        buf[p, 0:1, 0:nb] = s.bias_v[0:1, nb * d:nb * d + nb]
        buf[p, 0:1, nb:nb + ng] = s.gain_v[0:1, ng * d:ng * d + ng]


def layer_kernel(names, t, small_sizes, group_shape, lined, *refs):
    s = Names()
    for n, r in zip(names, refs, strict=True):
        setattr(s, n, r)
    D = s.x.shape[1]
    nb, ng = small_sizes
    s.small_sizes, s.group_shape, s.lined = small_sizes, group_shape, lined
    s.bias = lambda base, off, w: s.bias_v[0:1, base + off:base + off + w]
    s.gain = lambda base: s.gain_v[0:1, base:base + D]
    s.held = {n: getattr(s, "held_" + n) for n in ARRAYS}
    if lined:
        s.spare = {D // GROUPS * 3: s.spare_wide, D // GROUPS: s.spare_tall, D: None}
    t.locate()

    barrier = pltpu.get_barrier_semaphore()
    peers = t.peers()
    for peer in peers:
        pl.semaphore_signal(barrier, inc=1, device_id=peer, device_id_type=MESH)
    pl.semaphore_wait(barrier, len(peers))

    gather, scatter = {}, {}
    for i, n in enumerate(ARRAYS):
        make = (NearGather, NearScatter) if n in NEAR else (Gather, Scatter)
        gather[n] = make[0](t, getattr(s, "in_" + n), s.held[n],
                            [getattr(s, "g_" + k).at[i] for k in ("local", "s1", "r1", "s2", "r2", "s3", "r3")])
        scatter[n] = make[1](t, s.held[n], *[getattr(s, k + "_" + n) for k in ("ra", "rb", "rc")],
                             [getattr(s, "h_" + k).at[i] for k in ("s1", "r1", "s2", "r2", "s3", "r3")])
    near_first = t.nx == 2
    half = t.x if near_first else 0
    rest = 1 - half

    take_x = pltpu.make_async_copy(s.x_in, s.x, s.moves.at[0])
    take_cot = pltpu.make_async_copy(s.cot_in, s.cot, s.moves.at[1])
    give_out = pltpu.make_async_copy(s.out, s.out_to, s.moves.at[2])
    give_din = pltpu.make_async_copy(s.din, s.din_to, s.moves.at[3])

    gather["small"].begin()
    gather["qkv"].begin()
    take_x.start()
    take_cot.start()
    stage_mask(s)
    gather["small"].spread()
    gather["small"].share()
    gather["qkv"].spread()
    gather["out"].begin()
    gather["up"].begin()
    gather["down"].begin()
    gather["small"].near_done()
    gather["small"].far_done()
    assemble_small(s, t)
    take_x.wait()
    gather["qkv"].near_done()
    if not near_first:
        gather["qkv"].share()
        gather["qkv"].far_done()
    assemble_qkv(s, t, half)
    stage_qkv(s, half)
    stage_attn_fwd(s, 3 * half, 3 * half + 1)
    gather["out"].spread()
    stage_attn_fwd(s, 3 * half + 1, 3 * half + 2)
    if near_first:
        gather["qkv"].share()
    gather["up"].spread()
    stage_attn_fwd(s, 3 * half + 2, 3 * half + 3)
    gather["down"].spread()
    if near_first:
        gather["qkv"].far_done()
    assemble_qkv(s, t, rest)
    stage_qkv(s, rest)
    stage_attn_fwd(s, 3 * rest, 3 * rest + 1)
    gather["out"].share()
    stage_attn_fwd(s, 3 * rest + 1, 3 * rest + 2)
    gather["out"].share_last()
    gather["up"].share()
    stage_attn_fwd(s, 3 * rest + 2, 3 * rest + 3)
    gather["down"].share()
    gather["out"].done()
    assemble(s, t, "out")
    gather["up"].share_last()
    stage_ln1(s)
    gather["down"].share_last()
    gather["up"].done()
    assemble(s, t, "up")
    gather["down"].done()
    assemble(s, t, "down")
    for n in ARRAYS:
        gather[n].close()
    stage_ffn(s)
    take_cot.wait()
    stage_ln2(s)
    give_out.start()

    def put(name):
        return lambda g, v: lay_out(s, t, name, group_places(t, g, g // 2, g % 2), v)

    stage_down_grad(s, put("down"))
    scatter["down"].begin()
    stage_ffn_back(s, 0, 2)
    scatter["down"].planes()
    stage_ffn_back(s, 2, 4)
    stage_up_grad(s, put("up"))
    scatter["up"].begin()
    stage_ln1_back(s)
    scatter["up"].planes()
    def put_out(v):
        gw = D // GROUPS
        for g in range(GROUPS):
            put("out")(g, v[g * gw:(g + 1) * gw])
    stage_out_grad(s, put_out)
    scatter["out"].begin()
    scatter["down"].planes_last()
    stage_attn_back(s, 3 * rest, 3 * rest + 1)
    scatter["out"].planes()
    stage_attn_back(s, 3 * rest + 1, 3 * rest + 2)
    scatter["up"].planes_last()
    stage_attn_back(s, 3 * rest + 2, 3 * rest + 3)
    scatter["down"].line()
    put_qkv = lambda h: lambda g, i, v: lay_out(s, t, "qkv", group_places(t, g, h, i), v)
    stage_qkv_grad(s, rest, put_qkv(rest))
    if near_first:
        scatter["qkv"].begin_far()
    stage_attn_back(s, 3 * half, 3 * half + 1)
    if near_first:
        scatter["qkv"].far()
    scatter["out"].planes_last()
    stage_attn_back(s, 3 * half + 1, 3 * half + 2)
    scatter["up"].line()
    s.grad_down[...] = scatter["down"].total()
    stage_attn_back(s, 3 * half + 2, 3 * half + 3)
    scatter["out"].line()
    stage_qkv_grad(s, half, put_qkv(half))
    if not near_first:
        scatter["qkv"].begin_far()
        scatter["qkv"].far()
    scatter["qkv"].begin_near()
    lay_out_small(s, t)
    scatter["small"].begin_far()
    scatter["small"].begin_near()
    scatter["qkv"].near()
    scatter["small"].far()
    stage_input_grad(s)
    give_din.start()
    scatter["small"].near()
    s.grad_up[...] = scatter["up"].total()
    s.grad_out[...] = scatter["out"].total()
    s.grad_qkv[...] = scatter["qkv"].total()
    small = scatter["small"].total()
    s.grad_bias[...] = small[:, 0:nb]
    s.grad_gain[...] = small[:, nb:nb + ng]
    give_out.wait()
    give_din.wait()
    for n in ARRAYS:
        scatter[n].close()


def hand_on(count, *refs):
    held, sems = refs[2 * count:3 * count], refs[3 * count]
    taken = [pltpu.make_async_copy(refs[i], held[i], sems.at[0, i]) for i in range(count)]
    given = [pltpu.make_async_copy(held[i], refs[count + i], sems.at[1, i]) for i in range(count)]
    for c in taken:
        c.start()
    for i in range(count):
        taken[i].wait()
        given[i].start()
    for c in given:
        c.wait()


def body(sizes, hidden_in, segment_ids, positions, token_mask, cotangent, qkv_weight, out_weight, up_weight, down_weight, biases, gains):
    rows, T, D = hidden_in.shape
    assert rows == 1
    gw, fg = D // GROUPS, FF // GROUPS
    t = Torus(sizes)
    nb, ng = biases.shape[0], gains.shape[0]
    depth = D // t.count
    group_shape = {"qkv": (gw, 3 * gw), "out": (gw, D), "up": (gw, fg), "down": (fg, gw)}
    lined = all(v.shape[0] % 512 == 0 for v in (qkv_weight, out_weight, up_weight, down_weight))
    blocks = {"small": ((1, nb + ng), f32)}
    for n, flat in zip(ARRAYS[1:], (qkv_weight, out_weight, up_weight, down_weight)):
        size = flat.shape[0]
        blocks[n] = ((size // 128, 128) if lined else (size // group_shape[n][1], group_shape[n][1]), bf16)
    inputs = {
        "x_in": hidden_in[0], "seg": segment_ids, "pos": positions, "tok": token_mask, "cot_in": cotangent[0],
        "in_small": jnp.concatenate([biases, gains]).astype(f32).reshape(1, nb + ng),
        "in_qkv": qkv_weight.reshape(blocks["qkv"][0]),
        "in_out": out_weight.reshape(blocks["out"][0]),
        "in_up": up_weight.reshape(blocks["up"][0]),
        "in_down": down_weight.reshape(blocks["down"][0]),
    }
    outputs = {"out_to": ((T, D), bf16), "din_to": ((T, D), f32)}
    for n in ARRAYS[1:]:
        outputs["grad_" + n] = (blocks[n][0], f32)
    outputs["grad_bias"] = ((1, nb), f32)
    outputs["grad_gain"] = ((1, ng), f32)
    scratch = dict(
        x=((T, D), bf16), cot=((T, D), bf16), out=((T, D), bf16), din=((T, D), f32),
        mask=((T, T), f32), q=((T, D), bf16), k=((T, D), bf16), v=((T, D), bf16), pT=((HEADS, T, T), bf16),
        ctx=((T, D), bf16), ctxT=((D, T), bf16), att=((T, D), f32), n1=((T, D), f32), r1=((T, 128), f32),
        first_low=((T, D), bf16), active=((T, FF), bf16), gp=((T, FF), f32), dsec=((T, D), f32),
        douter=((T, D), bf16), dinner=((T, FF), bf16), dattn=((T, D), bf16), dctx=((T, D), bf16),
        dq=((T, D), bf16), dk=((T, D), bf16), dv=((T, D), bf16), joined=((GROUPS, T, 3 * gw), bf16),
        acc_g2=((8, D), f32), acc_s2=((8, D), f32), acc_down=((8, D), f32), acc_up=((8, FF), f32),
        acc_g1=((8, D), f32), acc_s1=((8, D), f32), acc_out=((8, D), f32),
        bias_v=((1, nb * t.count), f32), gain_v=((1, ng * t.count), f32),
        wqkv=((GROUPS, gw, 3 * gw), bf16), wout=((D, D), bf16), wup=((GROUPS, gw, fg), bf16),
        wdown=((GROUPS, fg, gw), bf16),
    )
    if lined:
        scratch["lines"] = ((fg * gw // 128, 128), f32)
        scratch["spare_wide"] = ((3 * gw // 128 + 1, gw, 128), f32)
        scratch["spare_tall"] = ((gw // 128 + 1, fg, 128), f32)
    planes = t.nx * t.ny
    for n in ARRAYS:
        shape, kind = blocks[n]
        scratch["held_" + n] = ((t.count,) + shape, kind)
        near = n in NEAR
        scratch["ra_" + n] = ((t.nx, t.flat) if near else (planes, t.nz)) + shape, kind
        scratch["rb_" + n] = ((t.nx, t.flat) if near else (planes - 1, t.nz)) + shape, kind
        scratch["rc_" + n] = ((t.flat - 1,) if near else (t.nz,)) + shape, kind
    shapes = [pltpu.VMEM(*scratch[n]) for n in scratch]
    most = max(planes, t.flat)
    sems = ["g_local", "g_s1", "g_r1", "g_s2", "g_r2", "g_s3", "g_r3", "h_s1", "h_r1", "h_s2", "h_r2", "h_s3", "h_r3"]
    shapes += [pltpu.SemaphoreType.DMA((len(ARRAYS), most)) for n in sems]
    shapes.append(pltpu.SemaphoreType.DMA((4,)))
    names = list(inputs) + list(outputs) + list(scratch) + list(sems) + ["moves"]
    vm = pl.BlockSpec(memory_space=pltpu.VMEM)
    anywhere = pl.BlockSpec(memory_space=pl.ANY)
    found = pl.pallas_call(
        lambda *refs: layer_kernel(names, t, (nb, ng), group_shape, lined, *refs),
        out_shape=[jax.ShapeDtypeStruct(*outputs[n]) for n in outputs],
        in_specs=[anywhere if n in ("x_in", "cot_in") else vm for n in inputs],
        out_specs=[anywhere if n in ("out_to", "din_to") else vm for n in outputs],
        scratch_shapes=shapes,
        compiler_params=pltpu.CompilerParams(
            collective_id=0, has_side_effects=True, vmem_limit_bytes=67043328
        ),
        name="layer",
    )(*inputs.values())
    count = len(outputs)
    found = pl.pallas_call(
        lambda *refs: hand_on(count, *refs),
        out_shape=[jax.ShapeDtypeStruct(*outputs[n]) for n in outputs],
        in_specs=[anywhere] * count,
        out_specs=[anywhere] * count,
        scratch_shapes=[pltpu.VMEM(*outputs[n]) for n in outputs] + [pltpu.SemaphoreType.DMA((2, count))],
        name="hand_on",
    )(*found)
    o = dict(zip(outputs, found))
    return (
        o["out_to"][None], o["din_to"][None], o["grad_qkv"].reshape(-1), o["grad_out"].reshape(-1), o["grad_up"].reshape(-1),
        o["grad_down"].reshape(-1), o["grad_bias"].reshape(-1), o["grad_gain"].reshape(-1),
    )


def solution(mesh):
    whole = P(("gx", "gy"))
    rows2 = P(("gx", "gy"), None)
    rows3 = P(("gx", "gy"), None, None)
    sizes = (mesh.shape["gx"], mesh.shape["gy"])
    return jax.shard_map(
        lambda *args: body(sizes, *args),
        mesh=mesh,
        in_specs=(rows3, rows2, rows2, rows2, rows3) + (whole,) * 6,
        out_specs=(rows3, rows3) + (whole,) * 6,
        check_vma=False,
    )
```

```python
import jax
import jax.numpy as jnp
from jax import lax
from jax.experimental import pallas as pl
from jax.experimental.pallas import tpu as pltpu
from jax.sharding import PartitionSpec as P

FF = 3072
HEADS = 12
GROUPS = 4
epsilon = 1e-05
f32 = jnp.float32
bf16 = jnp.bfloat16


def dot(a, b):
    return lax.dot_general(a, b, (((1,), (0,)), ((), ())), preferred_element_type=f32)

def dot_nt(a, b):
    return lax.dot_general(a, b, (((1,), (1,)), ((), ())), preferred_element_type=f32)

def dot_tn(a, b):
    return lax.dot_general(a, b, (((0,), (0,)), ((), ())), preferred_element_type=f32)

def fold(v):
    return jnp.sum(v.reshape(v.shape[0] // 8, 8, v.shape[1]), axis=0)


def stage_qkv(s, half):
    T, D = s.x.shape
    gw = D // GROUPS
    cols = pl.ds(pl.multiple_of(half * 2 * gw, 128), 2 * gw)
    value_cols = pl.ds(pl.multiple_of(half * 2 * gw + D, 128), 2 * gw)
    xh = s.x[:, cols]
    parts = [dot(xh[:, i * gw:(i + 1) * gw], s.wqkv[2 * half + i]) for i in range(2)]
    def both(i):
        return jnp.concatenate([parts[0][:, i * gw:(i + 1) * gw], parts[1][:, i * gw:(i + 1) * gw]], axis=1)
    s.q[:, cols] = (both(0) + s.bias_v[0:1, cols]).astype(bf16) * jnp.asarray(0.125, bf16)
    s.k[:, cols] = both(1).astype(bf16)
    s.v[:, cols] = (both(2) + s.bias_v[0:1, value_cols]).astype(bf16)


def stage_mask(s):
    T, D = s.x.shape
    place = lax.broadcasted_iota(jnp.int32, (1, T), 1)
    code = s.seg[...] * 1024 + (place - s.pos[...])
    keyed = jnp.where(s.tok[...] == 1, code, -1)
    keyed = jnp.broadcast_to(keyed.astype(f32), (128, T)).T
    code_f = code.astype(f32)
    for c in range(T // 128):
        cols = pl.ds(c * 128, 128)
        same = keyed == code_f[:, c * 128:(c + 1) * 128]
        rows = lax.broadcasted_iota(jnp.int32, (T, 128), 0)
        lanes = lax.broadcasted_iota(jnp.int32, (T, 128), 1) + c * 128
        s.mask[:, cols] = jnp.where(same | (rows == lanes), 0.0, -1000000000.0)


def stage_attn_fwd(s, lo, hi):
    T, D = s.x.shape
    lane = lax.broadcasted_iota(jnp.int32, (1, 128), 1)
    def pair_step(pr, carry):
        cols = pl.ds(pl.multiple_of(pr * 128, 128), 128)
        q2 = s.q[:, cols]
        k2 = s.k[:, cols]
        vT = s.v[:, cols].T
        outs = []
        for h in range(2):
            keep = (lane < 64) if h == 0 else (lane >= 64)
            qm = jnp.where(keep, q2, jnp.zeros_like(q2))
            sT = dot_nt(k2, qm) + s.mask[...]
            m = jnp.max(sT, axis=0, keepdims=True)
            e = jnp.exp(sT - m)
            l = jnp.sum(e, axis=0, keepdims=True)
            p = (e * (1.0 / l)).astype(bf16)
            s.pT[2 * pr + h] = p
            outs.append(dot(vT[64 * h:64 * h + 64], p))
        cT = jnp.concatenate(outs, axis=0).astype(bf16)
        s.ctxT[pl.ds(pl.multiple_of(pr * 128, 128), 128), :] = cT
        s.ctx[:, cols] = cT.T
        return carry
    lax.fori_loop(lo, hi, pair_step, 0)


def stage_ln1(s):
    T, D = s.x.shape
    s.att[...] = dot(s.ctx[...], s.wout[...])
    R = 32
    def step(i, carry):
        rows = pl.ds(pl.multiple_of(i * R, R), R)
        u = s.x[rows, :].astype(f32) + (s.att[rows, :] + s.bias(2 * D, 0, D))
        c = u - jnp.sum(u, axis=1, keepdims=True) * (1.0 / D)
        r = lax.rsqrt(jnp.sum(c * c, axis=1, keepdims=True) * (1.0 / D) + epsilon)
        n = c * r
        s.n1[rows, :] = n
        s.r1[rows, :] = jnp.broadcast_to(r, (R, 128))
        s.first_low[rows, :] = (n * s.gain(0) + s.bias(3 * D, 0, D)).astype(bf16)
        return carry
    lax.fori_loop(0, T // R, step, 0)


def gelu_parts(z):
    phi = 0.5 * (1.0 + lax.erf(z * 0.7071067811865476))
    dens = jnp.exp(z * z * -0.5) * 0.3989422804014327
    return z * phi, phi + z * dens


def stage_ffn(s):
    T, D = s.x.shape
    gw, fg = D // GROUPS, FF // GROUPS
    R = 128
    def step(i, carry):
        rows = pl.ds(pl.multiple_of(i * R, R), R)
        for pair in range(2):
            outs = []
            for g in (2 * pair, 2 * pair + 1):
                z = dot(s.first_low[rows, g * gw:(g + 1) * gw], s.wup[g]) + s.bias(4 * D, g * fg, fg)
                act, gp = gelu_parts(z)
                act = act.astype(bf16)
                s.active[rows, g * fg:(g + 1) * fg] = act
                s.gp[rows, g * fg:(g + 1) * fg] = gp
                outs.append(dot(act, s.wdown[g]))
            s.att[rows, pair * 2 * gw:(pair + 1) * 2 * gw] = jnp.concatenate(outs, axis=1)
        return carry
    lax.fori_loop(0, T // R, step, 0)


def stage_ln2(s):
    T, D = s.x.shape
    R = 32
    for a in (s.acc_g2, s.acc_s2, s.acc_down):
        a[...] = jnp.zeros_like(a)
    def step(i, carry):
        rows = pl.ds(pl.multiple_of(i * R, R), R)
        first = s.n1[rows, :] * s.gain(0) + s.bias(3 * D, 0, D)
        u = first + (s.att[rows, :] + s.bias(4 * D + FF, 0, D))
        c = u - jnp.sum(u, axis=1, keepdims=True) * (1.0 / D)
        r = lax.rsqrt(jnp.sum(c * c, axis=1, keepdims=True) * (1.0 / D) + epsilon)
        n = c * r
        s.out[rows, :] = (n * s.gain(D) + s.bias(5 * D + FF, 0, D)).astype(bf16)
        dy = s.cot[rows, :].astype(f32)
        s.acc_g2[...] += fold(dy * n)
        s.acc_s2[...] += fold(dy)
        e = dy * s.gain(D)
        m1 = jnp.sum(e, axis=1, keepdims=True) * (1.0 / D)
        m2 = jnp.sum(e * n, axis=1, keepdims=True) * (1.0 / D)
        du = r * (e - m1 - n * m2)
        s.dsec[rows, :] = du
        dl = du.astype(bf16)
        s.douter[rows, :] = dl
        s.acc_down[...] += fold(dl.astype(f32))
        return carry
    lax.fori_loop(0, T // R, step, 0)


def stage_ffn_back(s, lo, hi):
    T, D = s.x.shape
    gw, fg = D // GROUPS, FF // GROUPS
    R = 128
    if lo == 0:
        s.acc_up[...] = jnp.zeros_like(s.acc_up)
    def step(i, carry):
        rows = pl.ds(pl.multiple_of(i * R, R), R)
        for pair in range(2):
            outs = []
            for g in (2 * pair, 2 * pair + 1):
                da = dot_nt(s.douter[rows, g * gw:(g + 1) * gw], s.wdown[g])
                di = (da * s.gp[rows, g * fg:(g + 1) * fg]).astype(bf16)
                s.dinner[rows, g * fg:(g + 1) * fg] = di
                s.acc_up[:, g * fg:(g + 1) * fg] += fold(di.astype(f32))
                outs.append(dot_nt(di, s.wup[g]))
            s.att[rows, pair * 2 * gw:(pair + 1) * 2 * gw] = jnp.concatenate(outs, axis=1)
        return carry
    lax.fori_loop(T // R * lo // 4, T // R * hi // 4, step, 0)


def stage_down_grad(s, put):
    T, D = s.x.shape
    gw, fg = D // GROUPS, FF // GROUPS
    for g in range(GROUPS):
        put(g, dot_tn(s.active[:, g * fg:(g + 1) * fg], s.douter[:, g * gw:(g + 1) * gw]))


def stage_up_grad(s, put):
    T, D = s.x.shape
    gw, fg = D // GROUPS, FF // GROUPS
    for g in range(GROUPS):
        put(g, dot_tn(s.first_low[:, g * gw:(g + 1) * gw], s.dinner[:, g * fg:(g + 1) * fg]))


def stage_ln1_back(s):
    T, D = s.x.shape
    R = 32
    for a in (s.acc_g1, s.acc_s1, s.acc_out):
        a[...] = jnp.zeros_like(a)
    def step(i, carry):
        rows = pl.ds(pl.multiple_of(i * R, R), R)
        dy = s.dsec[rows, :] + s.att[rows, :]
        n = s.n1[rows, :]
        s.acc_g1[...] += fold(dy * n)
        s.acc_s1[...] += fold(dy)
        e = dy * s.gain(0)
        m1 = jnp.sum(e, axis=1, keepdims=True) * (1.0 / D)
        m2 = jnp.sum(e * n, axis=1, keepdims=True) * (1.0 / D)
        du = s.r1[rows, 0:1] * (e - m1 - n * m2)
        s.dsec[rows, :] = du
        dl = du.astype(bf16)
        s.dattn[rows, :] = dl
        s.acc_out[...] += fold(dl.astype(f32))
        return carry
    lax.fori_loop(0, T // R, step, 0)


def stage_out_grad(s, put):
    put(dot(s.ctxT[...], s.dattn[...]))
    s.dctx[...] = dot_nt(s.dattn[...], s.wout[...]).astype(bf16)


def stage_attn_back(s, lo, hi):
    T, D = s.x.shape
    lane = lax.broadcasted_iota(jnp.int32, (1, 128), 1)
    def pair_step(pr, carry):
        start = pl.multiple_of(pr * 128, 128)
        cols = pl.ds(start, 128)
        q2 = s.q[:, cols]
        v2 = s.v[:, cols]
        dc2 = s.dctx[:, cols]
        kT = s.k[:, cols].T
        prod = (s.ctxT[cols, :].astype(f32)) * (dc2.T.astype(f32))
        dk, dv, dqT = [], [], []
        for h in range(2):
            keep = (lane < 64) if h == 0 else (lane >= 64)
            qm = jnp.where(keep, q2, jnp.zeros_like(q2))
            dcm = jnp.where(keep, dc2, jnp.zeros_like(dc2))
            p = s.pT[2 * pr + h]
            delta = jnp.sum(prod[64 * h:64 * h + 64], axis=0, keepdims=True)
            dp = dot_nt(v2, dcm)
            ds = (p.astype(f32) * (dp - delta)).astype(bf16)
            dv.append(dot(p, dcm))
            dk.append(dot(ds, qm))
            dqT.append(dot(kT[64 * h:64 * h + 64], ds))
        s.dv[:, cols] = (dv[0] + dv[1]).astype(bf16)
        s.dk[:, cols] = (dk[0] + dk[1]).astype(bf16)
        s.dq[:, cols] = (jnp.concatenate(dqT, axis=0) * 0.125).astype(bf16).T
        return carry
    lax.fori_loop(lo, hi, pair_step, 0)


def stage_qkv_grad(s, half, put):
    T, D = s.x.shape
    gw = D // GROUPS
    cols = pl.ds(pl.multiple_of(half * 2 * gw, 128), 2 * gw)
    xh, dq, dk, dv = s.x[:, cols], s.dq[:, cols], s.dk[:, cols], s.dv[:, cols]
    for i in range(2):
        c = slice(i * gw, (i + 1) * gw)
        joined = jnp.concatenate([dq[:, c], dk[:, c], dv[:, c]], axis=1)
        s.joined[2 * half + i] = joined
        put(2 * half + i, i, dot_tn(xh[:, c], joined))


def stage_qkv_grad_one(s, half, i, put):
    T, D = s.x.shape
    gw = D // GROUPS
    cols = pl.ds(pl.multiple_of(half * 2 * gw, 128), 2 * gw)
    xh, dq, dk, dv = (lax.select_n(i == 0, v[:, gw:], v[:, :gw]) for v in (s.x[:, cols], s.dq[:, cols], s.dk[:, cols], s.dv[:, cols]))
    joined = jnp.concatenate([dq, dk, dv], axis=1)
    s.joined[2 * half + i] = joined
    put(2 * half + i, i, dot_tn(xh, joined))


def stage_input_grad(s):
    T, D = s.x.shape
    gw = D // GROUPS
    for pair in range(2):
        cols = slice(pair * 2 * gw, (pair + 1) * 2 * gw)
        outs = [dot_nt(s.joined[g], s.wqkv[g]) for g in (2 * pair, 2 * pair + 1)]
        s.din[:, cols] = s.dsec[:, cols] + jnp.concatenate(outs, axis=1)


MESH = pl.DeviceIdType.MESH
ARRAYS = ("small", "qkv", "out", "up", "down")
NEAR = ("small", "qkv")


class Names:
    pass


class Torus:
    def __init__(self, sizes):
        self.nx, gy = sizes
        self.nc = 2
        assert gy % self.nc == 0
        self.nz = 4 if (gy // self.nc) % 4 == 0 else 1
        self.ny = gy // self.nc // self.nz
        self.count = self.nx * gy
        self.square = self.nx == 2 and self.ny == 2
        self.flat = self.ny * self.nz
        self.near_first = self.nx == 2
        self.quads = self.near_first and self.nz == 4

    def locate(self):
        gy = lax.axis_index("gy")
        self.x = lax.axis_index("gx")
        self.c = gy % self.nc
        self.y = gy // self.nc % self.ny
        self.z = gy // (self.nc * self.ny)

    def device(self, x, y, z, c):
        return (x, (z * self.ny + y) * self.nc + c)

    def sibling(self):
        return self.device(self.x, self.y, self.z, 1 - self.c)

    def place(self, x, y, z, c):
        return ((c * self.nx + x) * self.ny + y) * self.nz + z

    def near_place(self, x, y, z, c):
        return ((c * self.nx + x) * self.nz + z) * self.ny + y

    def place_in(self, x, gy, near):
        place = self.near_place if near else self.place
        return place(x, gy // self.nc % self.ny, gy // (self.nc * self.ny), gy % self.nc)

    def place_of(self, index, near):
        gy_size = self.flat * self.nc
        return self.place_in(index // gy_size, index % gy_size, near)

    def shift(self, o):
        return (self.x + o[0]) % self.nx, (self.y + o[1]) % self.ny

    def turn(self, o):
        return (self.y + o[0]) % self.ny, (self.z + o[1]) % self.nz

    def plane_offsets(self):
        return [(i, j) for i in range(self.nx) for j in range(self.ny) if i or j]

    def flat_offsets(self):
        return [(i, j) for j in range(self.nz) for i in range(self.ny) if i or j]

    def peers(self):
        found = [self.device(self.x, y, z, self.c) for y, z in (self.turn(o) for o in self.flat_offsets())]
        for o in self.plane_offsets():
            if o[0] == 0 or (self.square and o == (1, 1)):
                continue
            px, py = self.shift(o)
            found.append(self.device(px, py, self.z, self.c))
        return found + [self.sibling()]


def remote(src, dst, send, recv, device):
    return pltpu.make_async_remote_copy(
        src_ref=src, dst_ref=dst, send_sem=send, recv_sem=recv, device_id=device, device_id_type=MESH
    )


class NearGather:
    def __init__(self, t, own, buf, sems):
        self.t, self.own, self.buf = t, own, buf
        self.local, self.s1, self.r1, self.s2, self.r2, self.s3, self.r3 = sems

    def chunk(self, x, c):
        return self.buf.at[pl.ds(self.t.near_place(x, 0, 0, c), self.t.flat)]

    def local_copy(self):
        t = self.t
        return pltpu.make_async_copy(self.own, self.buf.at[t.near_place(t.x, t.y, t.z, t.c)], self.local.at[0])

    def near_copies(self):
        t = self.t
        mine = self.buf.at[t.near_place(t.x, t.y, t.z, t.c)]
        found = []
        for k, o in enumerate(t.flat_offsets()):
            py, pz = t.turn(o)
            found.append(remote(self.own, mine, self.s1.at[k], self.r1.at[k], t.device(t.x, py, pz, t.c)))
        return found

    def far_copy(self, d):
        t = self.t
        part = self.chunk(t.x, t.c)
        return remote(part, part, self.s2.at[d], self.r2.at[d], t.device((t.x + d) % t.nx, t.y, t.z, t.c))

    def core_copy(self, d):
        t = self.t
        part = self.chunk((t.x + t.nx - d) % t.nx, t.c)
        return remote(part, part, self.s3.at[d], self.r3.at[d], t.sibling())

    def begin(self):
        self.local_copy().start()
        for c in self.near_copies():
            c.start()

    def spread(self):
        for c in self.near_copies():
            c.wait_recv()
        self.local_copy().wait()
        self.core_copy(0).start()
        for d in range(1, self.t.nx):
            self.far_copy(d).start()

    def near_done(self):
        self.core_copy(0).wait_recv()

    def share(self):
        for d in range(1, self.t.nx):
            self.far_copy(d).wait_recv()
            self.core_copy(d).start()

    def far_done(self):
        for d in range(1, self.t.nx):
            self.core_copy(d).wait_recv()

    def close(self):
        for c in self.near_copies():
            c.wait_send()
        for d in range(self.t.nx):
            self.core_copy(d).wait_send()
            if d:
                self.far_copy(d).wait_send()


class NearScatter:
    def __init__(self, t, buf, ra, rb, rc, sems):
        self.t, self.buf, self.ra, self.rb, self.rc = t, buf, ra, rb, rc
        self.s1, self.r1, self.s2, self.r2, self.s3, self.r3 = sems

    halves = False

    def turn(self, o):
        t = self.t
        if not self.halves:
            return t.turn(o)
        return (t.y + o[0]) % 2, (t.z // 2 + o[1]) % 2 * 2 + (t.z + o[2]) % 2

    def offsets(self):
        if not self.halves:
            return [self.t.flat_offsets()]
        return [[(i, a, b) for i in range(2) for b in range(2) if i or a or b] for a in range(2)]

    def far_core_copy(self, d):
        t = self.t
        part = self.buf.at[pl.ds(t.near_place((t.x + d) % t.nx, 0, 0, 1 - t.c), t.flat)]
        return remote(part, self.ra.at[d], self.s1.at[d], self.r1.at[d], t.sibling())

    def far_copy(self, d):
        t = self.t
        return remote(self.ra.at[d], self.rb.at[d], self.s2.at[d], self.r2.at[d],
                      t.device((t.x + d) % t.nx, t.y, t.z, t.c))

    def span(self, part):
        t = self.t
        if not self.halves:
            return 0, t.flat
        return (t.z // 2 + part) % 2 * 2 * t.ny, 2 * t.ny

    def core_copy(self, part):
        t = self.t
        start, n = self.span(part)
        k = part * t.nx
        return remote(self.buf.at[pl.ds(t.near_place(t.x, 0, 0, 1 - t.c) + start, n)], self.ra.at[0, pl.ds(start, n)],
                      self.s1.at[k], self.r1.at[k], t.sibling())

    def flat_copies(self, part):
        t = self.t
        lists = self.offsets()
        first = sum(len(l) for l in lists[:part])
        found = []
        for k, o in enumerate(lists[part]):
            py, pz = self.turn(o)
            found.append(remote(self.ra.at[0, pz * t.ny + py], self.rc.at[first + k], self.s3.at[first + k],
                                self.r3.at[first + k], t.device(t.x, py, pz, t.c)))
        return found

    def begin_far(self):
        for d in range(1, self.t.nx):
            self.far_core_copy(d).start()

    def far(self):
        t = self.t
        for d in range(1, t.nx):
            self.far_core_copy(d).wait_recv()
            part = self.buf[pl.ds(t.near_place((t.x + d) % t.nx, 0, 0, t.c), t.flat)]
            self.ra[d] = (part.astype(f32) + self.ra[d].astype(f32)).astype(self.ra.dtype)
            self.far_copy(d).start()

    def begin_near(self, part):
        self.core_copy(part).start()

    def near(self, part):
        t = self.t
        start, n = self.span(part)
        self.core_copy(part).wait_recv()
        if part == len(self.offsets()) - 1:
            for d in range(1, t.nx):
                self.far_copy(d).wait_recv()
        own = self.buf[pl.ds(t.near_place(t.x, 0, 0, t.c) + start, n)]
        total = own.astype(f32) + self.ra[0, pl.ds(start, n)].astype(f32)
        for d in range(1, t.nx):
            total = total + self.rb[d, pl.ds(start, n)].astype(f32)
        self.ra[0, pl.ds(start, n)] = total.astype(self.ra.dtype)
        for c in self.flat_copies(part):
            c.start()

    def total(self):
        t = self.t
        total = self.ra[0, t.z * t.ny + t.y].astype(f32)
        k = 0
        for part in range(len(self.offsets())):
            for c in self.flat_copies(part):
                c.wait_recv()
                total = total + self.rc[k].astype(f32)
                k += 1
        return total

    def close(self):
        t = self.t
        for part in range(len(self.offsets())):
            self.core_copy(part).wait_send()
            for c in self.flat_copies(part):
                c.wait_send()
        for d in range(1, t.nx):
            self.far_core_copy(d).wait_send()
            self.far_copy(d).wait_send()


class Planes:
    def route(self):
        t = self.t
        if t.square:
            self.offsets = [(t.c, 1 - t.c), (1 - t.c, t.c)]
        else:
            self.offsets = t.plane_offsets()

    def slot(self, o):
        return o[0] * self.t.ny + o[1]

    def to(self, o):
        px, py = self.t.shift(o)
        return self.t.device(px, py, self.t.z, self.t.c)


class Gather(Planes):
    def __init__(self, t, own, buf, sems):
        self.t, self.own, self.buf = t, own, buf
        self.local, self.s1, self.r1, self.s2, self.r2, self.s3, self.r3 = sems
        self.route()

    def chunk(self, x, y):
        return self.buf.at[pl.ds(self.t.place(x, y, 0, self.t.c), self.t.nz)]

    def local_copy(self):
        t = self.t
        return pltpu.make_async_copy(self.own, self.buf.at[t.place(t.x, t.y, t.z, t.c)], self.local.at[0])

    def line_copies(self):
        t = self.t
        mine = self.buf.at[t.place(t.x, t.y, t.z, t.c)]
        return [
            remote(self.own, mine, self.s1.at[d], self.r1.at[d], t.device(t.x, t.y, (t.z + d) % t.nz, t.c))
            for d in range(1, t.nz)
        ]

    def plane_copy(self, k):
        part = self.chunk(self.t.x, self.t.y)
        return remote(part, part, self.s2.at[k], self.r2.at[k], self.to(self.offsets[k]))

    def relay_copy(self):
        part = self.chunk(*self.t.shift(self.offsets[0]))
        return remote(part, part, self.s2.at[2], self.r2.at[2], self.to(self.offsets[1]))

    def core_copy(self, o):
        t = self.t
        part = self.chunk((t.x + t.nx - o[0]) % t.nx, (t.y + t.ny - o[1]) % t.ny)
        k = self.slot(o)
        return remote(part, part, self.s3.at[k], self.r3.at[k], t.sibling())

    def begin(self):
        self.local_copy().start()
        for c in self.line_copies():
            c.start()

    def spread(self):
        for c in self.line_copies():
            c.wait_recv()
        self.local_copy().wait()
        for k in range(len(self.offsets)):
            self.plane_copy(k).start()
        self.core_copy((0, 0)).start()

    def share(self):
        for k, o in enumerate(self.offsets):
            self.plane_copy(k).wait_recv()
            if self.t.square and k == 0:
                self.relay_copy().start()
            self.core_copy(o).start()

    def share_last(self):
        if self.t.square:
            self.relay_copy().wait_recv()
            self.core_copy((1, 1)).start()

    def done(self):
        for o in [(0, 0)] + self.t.plane_offsets():
            self.core_copy(o).wait_recv()

    def close(self):
        for c in self.line_copies():
            c.wait_send()
        for k in range(len(self.offsets)):
            self.plane_copy(k).wait_send()
        if self.t.square:
            self.relay_copy().wait_send()
        for o in [(0, 0)] + self.t.plane_offsets():
            self.core_copy(o).wait_send()


class Scatter(Planes):
    def __init__(self, t, buf, ra, rb, rc, sems):
        self.t, self.buf, self.ra, self.rb, self.rc = t, buf, ra, rb, rc
        self.s1, self.r1, self.s2, self.r2, self.s3, self.r3 = sems
        self.route()

    def core_copy(self, o):
        t = self.t
        px, py = t.shift(o)
        part = self.buf.at[pl.ds(t.place(px, py, 0, 1 - t.c), t.nz)]
        k = self.slot(o)
        return remote(part, self.ra.at[k], self.s1.at[k], self.r1.at[k], t.sibling())

    def plane_copy(self, k, o, to):
        return remote(self.ra.at[self.slot(o)], self.rb.at[k], self.s2.at[k], self.r2.at[k], self.to(to))

    def line_copy(self, d):
        t = self.t
        to = (t.z + d) % t.nz
        return remote(self.ra.at[0, to], self.rc.at[d], self.s3.at[d], self.r3.at[d], t.device(t.x, t.y, to, t.c))

    def hops(self):
        if self.t.square:
            a, b = self.offsets
            return [(0, (1, 1), b), (1, b, b), (2, a, a)]
        return [(k, o, o) for k, o in enumerate(self.offsets)]

    def chip_sum(self, o):
        t = self.t
        px, py = t.shift(o)
        part = self.buf[pl.ds(t.place(px, py, 0, t.c), t.nz)]
        return part.astype(f32) + self.ra[self.slot(o)].astype(f32)

    def begin(self):
        for o in self.t.plane_offsets() + [(0, 0)]:
            self.core_copy(o).start()

    def planes(self):
        for o in self.t.plane_offsets() + [(0, 0)]:
            self.core_copy(o).wait_recv()
        for k, o, to in self.hops()[:2] if self.t.square else self.hops():
            self.ra[self.slot(o)] = self.chip_sum(o).astype(self.ra.dtype)
            self.plane_copy(k, o, to).start()

    def planes_last(self):
        if self.t.square:
            hops = self.hops()
            self.plane_copy(*hops[0]).wait_recv()
            k, o, to = hops[2]
            self.ra[self.slot(o)] = (self.chip_sum(o) + self.rb[0].astype(f32)).astype(self.ra.dtype)
            self.plane_copy(k, o, to).start()

    def line(self):
        t = self.t
        total = self.chip_sum((0, 0))
        for k, o, to in self.hops()[1:] if t.square else self.hops():
            self.plane_copy(k, o, to).wait_recv()
            total = total + self.rb[k].astype(f32)
        self.ra[0] = total.astype(self.ra.dtype)
        for d in range(1, t.nz):
            self.line_copy(d).start()

    def total(self):
        t = self.t
        total = self.ra[0, t.z].astype(f32)
        for d in range(1, t.nz):
            self.line_copy(d).wait_recv()
            total = total + self.rc[d].astype(f32)
        return total

    def close(self):
        for d in range(1, self.t.nz):
            self.line_copy(d).wait_send()
        for hop in self.hops():
            self.plane_copy(*hop).wait_send()
        for o in self.t.plane_offsets() + [(0, 0)]:
            self.core_copy(o).wait_send()


def swap_halves(a, b):
    lane = lax.broadcasted_iota(jnp.int32, a.shape, 1)
    return jnp.where(lane < 64, pltpu.roll(a, 64, 1), pltpu.roll(b, 64, 1))


def lines_to_rows(lines, spare, rows, width):
    if width % 128 == 0:
        m = width // 128
        return jnp.concatenate([lines[pl.ds(j, rows, stride=m), :] for j in range(m)], axis=1).astype(bf16)
    m = width // 64
    q, half = m // 2, rows // 2
    a = [lines[pl.ds(j, half, stride=m), :] for j in range(m)]
    for j in range(q + 1):
        spare[j, pl.ds(0, half, stride=2), :] = a[j]
        spare[j, pl.ds(1, half, stride=2), :] = swap_halves(a[q + j], a[q + j + 1] if j < q else a[q + j])
    return jnp.concatenate([spare[j] for j in range(q)] + [spare[q][:, 0:64]], axis=1).astype(bf16)


def rows_to_lines(value, lines, spare):
    rows, width = value.shape
    if width % 128 == 0:
        m = width // 128
        for j in range(m):
            lines[pl.ds(j, rows, stride=m), :] = value[:, 128 * j:128 * j + 128]
        return
    m = width // 64
    q, half = m // 2, rows // 2
    for j in range(q):
        spare[j] = value[:, 128 * j:128 * j + 128]
    spare[q, :, 0:64] = value[:, 128 * q:width]
    even = [spare[j, pl.ds(0, half, stride=2), :] for j in range(q + 1)]
    odd = [spare[j, pl.ds(1, half, stride=2), :] for j in range(q + 1)]
    lane = lax.broadcasted_iota(jnp.int32, even[0].shape, 1)
    for j in range(q):
        lines[pl.ds(j, half, stride=m), :] = even[j]
        lines[pl.ds(q + 1 + j, half, stride=m), :] = swap_halves(odd[j], odd[j + 1])
    lines[pl.ds(q, half, stride=m), :] = jnp.where(lane < 64, even[q], pltpu.roll(odd[0], 64, 1))


def group_places(t, g, half, i, near):
    per = t.count // GROUPS
    if t.nx == 2:
        return [t.place_in(half, i * per + j, near) for j in range(per)]
    return [t.place_of(g * per + j, near) for j in range(per)]


def group_weight(s, t, name, places):
    buf = s.held[name]
    rows, width = s.group_shape[name]
    if s.lined:
        n = buf.shape[1]
        for j, p in enumerate(places):
            s.lines[n * j:n * j + n, :] = buf[p].astype(f32)
        return lines_to_rows(s.lines, s.spare[width], rows, width)
    return jnp.concatenate([buf[p].astype(f32) for p in places], axis=0).astype(bf16)


def assemble_small(s, t):
    nb, ng = s.small_sizes
    buf = s.held["small"]
    for d in range(t.count):
        p = t.place_of(d, True)
        s.bias_v[0:1, nb * d:nb * d + nb] = buf[p, 0:1, 0:nb]
        s.gain_v[0:1, ng * d:ng * d + ng] = buf[p, 0:1, nb:nb + ng]


def assemble_qkv(s, t, half):
    for i in range(2):
        g = 2 * half + i
        s.wqkv[g] = group_weight(s, t, "qkv", group_places(t, g, half, i, True))


def assemble(s, t, name):
    for g in range(GROUPS):
        value = group_weight(s, t, name, group_places(t, g, g // 2, g % 2, False))
        if name == "out":
            gw = s.wout.shape[0] // GROUPS
            s.wout[g * gw:(g + 1) * gw, :] = value
        elif name == "up":
            s.wup[g] = value
        else:
            s.wdown[g] = value


def lay_out(s, t, name, places, value):
    buf = s.held[name]
    if s.lined:
        n = buf.shape[1]
        rows_to_lines(value, s.lines, s.spare[value.shape[1]] if value.shape[1] % 128 else None)
        for j, p in enumerate(places):
            buf[p] = s.lines[n * j:n * j + n, :].astype(bf16)
        return
    rows = value.shape[0] // len(places)
    for j, p in enumerate(places):
        buf[p] = value[rows * j:rows * j + rows].astype(bf16)


def lay_out_small(s, t):
    T, D = s.x.shape
    nb, ng = s.small_sizes
    def rs(v):
        return jnp.sum(v, axis=0, keepdims=True)
    s.bias_v[:, 0:D] = rs(s.dq[...].astype(f32))
    s.bias_v[:, D:2 * D] = rs(s.dv[...].astype(f32))
    s.bias_v[:, 2 * D:3 * D] = rs(s.acc_out[...])
    s.bias_v[:, 3 * D:4 * D] = rs(s.acc_s1[...])
    s.bias_v[:, 4 * D:4 * D + FF] = rs(s.acc_up[...])
    s.bias_v[:, 4 * D + FF:5 * D + FF] = rs(s.acc_down[...])
    s.bias_v[:, 5 * D + FF:] = rs(s.acc_s2[...])
    s.gain_v[:, 0:D] = rs(s.acc_g1[...])
    s.gain_v[:, D:] = rs(s.acc_g2[...])
    buf = s.held["small"]
    for d in range(t.count):
        p = t.place_of(d, True)
        buf[p, 0:1, 0:nb] = s.bias_v[0:1, nb * d:nb * d + nb]
        buf[p, 0:1, nb:nb + ng] = s.gain_v[0:1, ng * d:ng * d + ng]


def layer_kernel(names, t, small_sizes, group_shape, lined, *refs):
    s = Names()
    for n, r in zip(names, refs, strict=True):
        setattr(s, n, r)
    D = s.x.shape[1]
    nb, ng = small_sizes
    s.small_sizes, s.group_shape, s.lined = small_sizes, group_shape, lined
    s.bias = lambda base, off, w: s.bias_v[0:1, base + off:base + off + w]
    s.gain = lambda base: s.gain_v[0:1, base:base + D]
    s.held = {n: getattr(s, "held_" + n) for n in ARRAYS}
    if lined:
        s.spare = {D // GROUPS * 3: s.spare_wide, D // GROUPS: s.spare_tall, D: None}
    t.locate()
    s.in_small[0:1, 0:nb] = s.in_bias[...].astype(f32).reshape(1, nb)
    s.in_small[0:1, nb:nb + ng] = s.in_gain[...].astype(f32).reshape(1, ng)

    barrier = pltpu.get_barrier_semaphore()
    peers = t.peers()
    for peer in peers:
        pl.semaphore_signal(barrier, inc=1, device_id=peer, device_id_type=MESH)
    pl.semaphore_wait(barrier, len(peers))

    gather, scatter = {}, {}
    for i, n in enumerate(ARRAYS):
        make = (NearGather, NearScatter) if n in NEAR else (Gather, Scatter)
        gather[n] = make[0](t, getattr(s, "in_" + n), s.held[n],
                            [getattr(s, "g_" + k).at[i] for k in ("local", "s1", "r1", "s2", "r2", "s3", "r3")])
        scatter[n] = make[1](t, s.held[n], *[getattr(s, k + "_" + n) for k in ("ra", "rb", "rc")],
                             [getattr(s, "h_" + k).at[i] for k in ("s1", "r1", "s2", "r2", "s3", "r3")])
    scatter["qkv"].halves = t.quads
    near_first = t.near_first
    half = t.x if near_first else 0
    rest = 1 - half

    take_x = pltpu.make_async_copy(s.x_in, s.x, s.moves.at[0])
    take_cot = pltpu.make_async_copy(s.cot_in, s.cot, s.moves.at[1])
    give_out = pltpu.make_async_copy(s.out, s.out_to, s.moves.at[2])
    give_din = pltpu.make_async_copy(s.din, s.din_to, s.moves.at[3])

    gather["small"].begin()
    gather["qkv"].begin()
    take_x.start()
    take_cot.start()
    stage_mask(s)
    gather["small"].spread()
    gather["small"].share()
    gather["out"].begin()
    gather["qkv"].spread()
    gather["up"].begin()
    gather["down"].begin()
    gather["small"].near_done()
    gather["small"].far_done()
    assemble_small(s, t)
    take_x.wait()
    gather["qkv"].near_done()
    if not near_first:
        gather["qkv"].share()
        gather["qkv"].far_done()
    assemble_qkv(s, t, half)
    stage_qkv(s, half)
    stage_attn_fwd(s, 3 * half, 3 * half + 1)
    gather["out"].spread()
    stage_attn_fwd(s, 3 * half + 1, 3 * half + 2)
    if near_first:
        gather["qkv"].share()
    stage_attn_fwd(s, 3 * half + 2, 3 * half + 3)
    gather["up"].spread()
    gather["out"].share()
    if near_first:
        gather["qkv"].far_done()
    assemble_qkv(s, t, rest)
    stage_qkv(s, rest)
    gather["down"].spread()
    stage_attn_fwd(s, 3 * rest, 3 * rest + 1)
    gather["out"].share_last()
    gather["up"].share()
    stage_attn_fwd(s, 3 * rest + 1, 3 * rest + 2)
    stage_attn_fwd(s, 3 * rest + 2, 3 * rest + 3)
    gather["out"].done()
    assemble(s, t, "out")
    gather["down"].share()
    stage_ln1(s)
    gather["up"].share_last()
    gather["down"].share_last()
    gather["up"].done()
    assemble(s, t, "up")
    gather["down"].done()
    assemble(s, t, "down")
    for n in ARRAYS:
        gather[n].close()
    stage_ffn(s)
    take_cot.wait()
    stage_ln2(s)
    give_out.start()

    def put(name):
        return lambda g, v: lay_out(s, t, name, group_places(t, g, g // 2, g % 2, False), v)

    stage_down_grad(s, put("down"))
    scatter["down"].begin()
    stage_ffn_back(s, 0, 2)
    scatter["down"].planes()
    stage_ffn_back(s, 2, 4)
    stage_up_grad(s, put("up"))
    scatter["up"].begin()
    stage_ln1_back(s)
    scatter["up"].planes()
    def put_out(v):
        gw = D // GROUPS
        for g in range(GROUPS):
            put("out")(g, v[g * gw:(g + 1) * gw])
    stage_out_grad(s, put_out)
    scatter["out"].begin()
    scatter["down"].planes_last()
    stage_attn_back(s, 3 * rest, 3 * rest + 1)
    scatter["out"].planes()
    stage_attn_back(s, 3 * rest + 1, 3 * rest + 2)
    scatter["up"].planes_last()
    stage_attn_back(s, 3 * rest + 2, 3 * rest + 3)
    scatter["down"].line()
    put_qkv = lambda h: lambda g, i, v: lay_out(s, t, "qkv", group_places(t, g, h, i, True), v)
    stage_qkv_grad(s, rest, put_qkv(rest))
    if near_first:
        scatter["qkv"].begin_far()
    zh = t.z // 2 if t.quads else 0
    first = 3 * half + (2 - 2 * zh if t.quads else 0)
    last = 3 * half + (2 * zh if t.quads else 2)
    stage_attn_back(s, first, first + 1)
    if near_first:
        scatter["qkv"].far()
    scatter["out"].planes_last()
    stage_attn_back(s, 3 * half + 1, 3 * half + 2)
    if t.quads:
        stage_qkv_grad_one(s, half, 1 - zh, put_qkv(half))
        scatter["qkv"].begin_near(1)
    scatter["up"].line()
    s.grad_down[...] = scatter["down"].total()
    stage_attn_back(s, last, last + 1)
    if t.quads:
        scatter["qkv"].near(1)
    lay_out_small(s, t)
    scatter["small"].begin_far()
    scatter["small"].begin_near(0)
    scatter["out"].line()
    if t.quads:
        stage_qkv_grad_one(s, half, zh, put_qkv(half))
    else:
        stage_qkv_grad(s, half, put_qkv(half))
    if not near_first:
        scatter["qkv"].begin_far()
        scatter["qkv"].far()
    scatter["qkv"].begin_near(0)
    scatter["small"].far()
    scatter["small"].near(0)
    scatter["qkv"].near(0)
    stage_input_grad(s)
    give_din.start()
    s.grad_up[...] = scatter["up"].total()
    s.grad_out[...] = scatter["out"].total()
    s.grad_qkv[...] = scatter["qkv"].total()
    small = scatter["small"].total()
    s.grad_bias[...] = small[:, 0:nb]
    s.grad_gain[...] = small[:, nb:nb + ng]
    give_out.wait()
    give_din.wait()
    for n in ARRAYS:
        scatter[n].close()


def hand_on(count, *refs):
    held, sems = refs[2 * count:3 * count], refs[3 * count]
    taken = [pltpu.make_async_copy(refs[i], held[i], sems.at[0, i]) for i in range(count)]
    given = [pltpu.make_async_copy(held[i], refs[count + i], sems.at[1, i]) for i in range(count)]
    for c in taken:
        c.start()
    for i in range(count):
        taken[i].wait()
        given[i].start()
    for c in given:
        c.wait()


def body(sizes, hidden_in, segment_ids, positions, token_mask, cotangent, qkv_weight, out_weight, up_weight, down_weight, biases, gains):
    rows, T, D = hidden_in.shape
    assert rows == 1
    gw, fg = D // GROUPS, FF // GROUPS
    t = Torus(sizes)
    nb, ng = biases.shape[0], gains.shape[0]
    depth = D // t.count
    group_shape = {"qkv": (gw, 3 * gw), "out": (gw, D), "up": (gw, fg), "down": (fg, gw)}
    lined = all(v.shape[0] % 512 == 0 for v in (qkv_weight, out_weight, up_weight, down_weight))
    blocks = {"small": ((1, nb + ng), f32)}
    for n, flat in zip(ARRAYS[1:], (qkv_weight, out_weight, up_weight, down_weight)):
        size = flat.shape[0]
        blocks[n] = ((size // 128, 128) if lined else (size // group_shape[n][1], group_shape[n][1]), bf16)
    inputs = {
        "x_in": hidden_in[0], "seg": segment_ids, "pos": positions, "tok": token_mask, "cot_in": cotangent[0],
        "in_bias": biases, "in_gain": gains,
        "in_qkv": qkv_weight.reshape(blocks["qkv"][0]),
        "in_out": out_weight.reshape(blocks["out"][0]),
        "in_up": up_weight.reshape(blocks["up"][0]),
        "in_down": down_weight.reshape(blocks["down"][0]),
    }
    outputs = {"out_to": ((T, D), bf16), "din_to": ((T, D), f32)}
    for n in ARRAYS[1:]:
        outputs["grad_" + n] = (blocks[n][0], f32)
    outputs["grad_bias"] = ((1, nb), f32)
    outputs["grad_gain"] = ((1, ng), f32)
    scratch = dict(
        x=((T, D), bf16), cot=((T, D), bf16), out=((T, D), bf16), din=((T, D), f32),
        mask=((T, T), f32), q=((T, D), bf16), k=((T, D), bf16), v=((T, D), bf16), pT=((HEADS, T, T), bf16),
        ctx=((T, D), bf16), ctxT=((D, T), bf16), att=((T, D), f32), n1=((T, D), f32), r1=((T, 128), f32),
        first_low=((T, D), bf16), active=((T, FF), bf16), gp=((T, FF), f32), dsec=((T, D), f32),
        douter=((T, D), bf16), dinner=((T, FF), bf16), dattn=((T, D), bf16), dctx=((T, D), bf16),
        dq=((T, D), bf16), dk=((T, D), bf16), dv=((T, D), bf16), joined=((GROUPS, T, 3 * gw), bf16),
        acc_g2=((8, D), f32), acc_s2=((8, D), f32), acc_down=((8, D), f32), acc_up=((8, FF), f32),
        acc_g1=((8, D), f32), acc_s1=((8, D), f32), acc_out=((8, D), f32),
        in_small=((1, nb + ng), f32), bias_v=((1, nb * t.count), f32), gain_v=((1, ng * t.count), f32),
        wqkv=((GROUPS, gw, 3 * gw), bf16), wout=((D, D), bf16), wup=((GROUPS, gw, fg), bf16),
        wdown=((GROUPS, fg, gw), bf16),
    )
    if lined:
        scratch["lines"] = ((fg * gw // 128, 128), f32)
        scratch["spare_wide"] = ((3 * gw // 128 + 1, gw, 128), f32)
        scratch["spare_tall"] = ((gw // 128 + 1, fg, 128), f32)
    planes = t.nx * t.ny
    for n in ARRAYS:
        shape, kind = blocks[n]
        scratch["held_" + n] = ((t.count,) + shape, kind)
        near = n in NEAR
        scratch["ra_" + n] = ((t.nx, t.flat) if near else (planes, t.nz)) + shape, kind
        scratch["rb_" + n] = ((t.nx, t.flat) if near else (planes - 1, t.nz)) + shape, kind
        scratch["rc_" + n] = ((t.flat - 1,) if near else (t.nz,)) + shape, kind
    shapes = [pltpu.VMEM(*scratch[n]) for n in scratch]
    most = max(planes, t.flat)
    sems = ["g_local", "g_s1", "g_r1", "g_s2", "g_r2", "g_s3", "g_r3", "h_s1", "h_r1", "h_s2", "h_r2", "h_s3", "h_r3"]
    shapes += [pltpu.SemaphoreType.DMA((len(ARRAYS), most)) for n in sems]
    shapes.append(pltpu.SemaphoreType.DMA((4,)))
    names = list(inputs) + list(outputs) + list(scratch) + list(sems) + ["moves"]
    vm = pl.BlockSpec(memory_space=pltpu.VMEM)
    anywhere = pl.BlockSpec(memory_space=pl.ANY)
    found = pl.pallas_call(
        lambda *refs: layer_kernel(names, t, (nb, ng), group_shape, lined, *refs),
        out_shape=[jax.ShapeDtypeStruct(*outputs[n]) for n in outputs],
        in_specs=[anywhere if n in ("x_in", "cot_in") else vm for n in inputs],
        out_specs=[anywhere if n in ("out_to", "din_to") else vm for n in outputs],
        scratch_shapes=shapes,
        compiler_params=pltpu.CompilerParams(
            collective_id=0, has_side_effects=True, vmem_limit_bytes=67043328
        ),
        name="layer",
    )(*inputs.values())
    count = len(outputs)
    found = pl.pallas_call(
        lambda *refs: hand_on(count, *refs),
        out_shape=[jax.ShapeDtypeStruct(*outputs[n]) for n in outputs],
        in_specs=[anywhere] * count,
        out_specs=[anywhere] * count,
        scratch_shapes=[pltpu.VMEM(*outputs[n]) for n in outputs] + [pltpu.SemaphoreType.DMA((2, count))],
        name="hand_on",
    )(*found)
    o = dict(zip(outputs, found))
    return (
        o["out_to"][None], o["din_to"][None], o["grad_qkv"].reshape(-1), o["grad_out"].reshape(-1), o["grad_up"].reshape(-1),
        o["grad_down"].reshape(-1), o["grad_bias"].reshape(-1), o["grad_gain"].reshape(-1),
    )


def solution(mesh):
    whole = P(("gx", "gy"))
    rows2 = P(("gx", "gy"), None)
    rows3 = P(("gx", "gy"), None, None)
    sizes = (mesh.shape["gx"], mesh.shape["gy"])
    return jax.shard_map(
        lambda *args: body(sizes, *args),
        mesh=mesh,
        in_specs=(rows3, rows2, rows2, rows2, rows3) + (whole,) * 6,
        out_specs=(rows3, rows3) + (whole,) * 6,
        check_vma=False,
    )
```

```python
import jax
import jax.numpy as jnp
from jax import lax
from jax.experimental import pallas as pl
from jax.experimental.pallas import tpu as pltpu
from jax.sharding import PartitionSpec as P

FF = 3072
HEADS = 12
GROUPS = 4
epsilon = 1e-05
f32 = jnp.float32
bf16 = jnp.bfloat16


def dot(a, b):
    return lax.dot_general(a, b, (((1,), (0,)), ((), ())), preferred_element_type=f32)

def dot_nt(a, b):
    return lax.dot_general(a, b, (((1,), (1,)), ((), ())), preferred_element_type=f32)

def dot_tn(a, b):
    return lax.dot_general(a, b, (((0,), (0,)), ((), ())), preferred_element_type=f32)

def fold(v):
    return jnp.sum(v.reshape(v.shape[0] // 8, 8, v.shape[1]), axis=0)


def stage_qkv(s, half):
    T, D = s.x.shape
    gw = D // GROUPS
    cols = pl.ds(pl.multiple_of(half * 2 * gw, 128), 2 * gw)
    value_cols = pl.ds(pl.multiple_of(half * 2 * gw + D, 128), 2 * gw)
    xh = s.x[:, cols]
    parts = [dot(xh[:, i * gw:(i + 1) * gw], s.wqkv[2 * half + i]) for i in range(2)]
    def both(i):
        return jnp.concatenate([parts[0][:, i * gw:(i + 1) * gw], parts[1][:, i * gw:(i + 1) * gw]], axis=1)
    s.q[:, cols] = (both(0) + s.bias_v[0:1, cols]).astype(bf16) * jnp.asarray(0.125, bf16)
    s.k[:, cols] = both(1).astype(bf16)
    s.v[:, cols] = (both(2) + s.bias_v[0:1, value_cols]).astype(bf16)


def stage_mask(s):
    T, D = s.x.shape
    place = lax.broadcasted_iota(jnp.int32, (1, T), 1)
    code = s.seg[...] * 1024 + (place - s.pos[...])
    keyed = jnp.where(s.tok[...] == 1, code, -1)
    keyed = jnp.broadcast_to(keyed.astype(f32), (128, T)).T
    code_f = code.astype(f32)
    for c in range(T // 128):
        cols = pl.ds(c * 128, 128)
        same = keyed == code_f[:, c * 128:(c + 1) * 128]
        rows = lax.broadcasted_iota(jnp.int32, (T, 128), 0)
        lanes = lax.broadcasted_iota(jnp.int32, (T, 128), 1) + c * 128
        s.mask[:, cols] = jnp.where(same | (rows == lanes), 0.0, -1000000000.0)


def stage_attn_fwd(s, lo, hi):
    T, D = s.x.shape
    lane = lax.broadcasted_iota(jnp.int32, (1, 128), 1)
    def pair_step(pr, carry):
        cols = pl.ds(pl.multiple_of(pr * 128, 128), 128)
        q2 = s.q[:, cols]
        k2 = s.k[:, cols]
        vT = s.v[:, cols].T
        outs = []
        for h in range(2):
            keep = (lane < 64) if h == 0 else (lane >= 64)
            qm = jnp.where(keep, q2, jnp.zeros_like(q2))
            sT = dot_nt(k2, qm) + s.mask[...]
            m = jnp.max(sT, axis=0, keepdims=True)
            e = jnp.exp(sT - m)
            l = jnp.sum(e, axis=0, keepdims=True)
            p = (e * (1.0 / l)).astype(bf16)
            s.pT[2 * pr + h] = p
            outs.append(dot(vT[64 * h:64 * h + 64], p))
        cT = jnp.concatenate(outs, axis=0).astype(bf16)
        s.ctxT[pl.ds(pl.multiple_of(pr * 128, 128), 128), :] = cT
        s.ctx[:, cols] = cT.T
        return carry
    lax.fori_loop(lo, hi, pair_step, 0)


def stage_ln1(s):
    T, D = s.x.shape
    s.att[...] = dot(s.ctx[...], s.wout[...])
    R = 128
    def step(i, carry):
        rows = pl.ds(pl.multiple_of(i * R, R), R)
        u = s.x[rows, :].astype(f32) + (s.att[rows, :] + s.bias(2 * D, 0, D))
        c = u - jnp.sum(u, axis=1, keepdims=True) * (1.0 / D)
        r = lax.rsqrt(jnp.sum(c * c, axis=1, keepdims=True) * (1.0 / D) + epsilon)
        n = c * r
        s.n1[rows, :] = n
        s.r1[rows, :] = jnp.broadcast_to(r, (R, 128))
        s.first_low[rows, :] = (n * s.gain(0) + s.bias(3 * D, 0, D)).astype(bf16)
        return carry
    lax.fori_loop(0, T // R, step, 0)


def gelu_parts(z):
    phi = 0.5 * (1.0 + lax.erf(z * 0.7071067811865476))
    dens = jnp.exp(z * z * -0.5) * 0.3989422804014327
    return z * phi, phi + z * dens


def stage_ffn(s):
    T, D = s.x.shape
    gw, fg = D // GROUPS, FF // GROUPS
    R = 256
    def step(i, carry):
        rows = pl.ds(pl.multiple_of(i * R, R), R)
        for pair in range(2):
            outs = []
            for g in (2 * pair, 2 * pair + 1):
                z = dot(s.first_low[rows, g * gw:(g + 1) * gw], s.wup[g]) + s.bias(4 * D, g * fg, fg)
                act, gp = gelu_parts(z)
                act = act.astype(bf16)
                s.active[rows, g * fg:(g + 1) * fg] = act
                s.gp[rows, g * fg:(g + 1) * fg] = gp
                outs.append(dot(act, s.wdown[g]))
            s.att[rows, pair * 2 * gw:(pair + 1) * 2 * gw] = jnp.concatenate(outs, axis=1)
        return carry
    lax.fori_loop(0, T // R, step, 0)


def stage_ln2(s):
    T, D = s.x.shape
    R = 128
    for a in (s.acc_g2, s.acc_s2, s.acc_down):
        a[...] = jnp.zeros_like(a)
    def step(i, carry):
        rows = pl.ds(pl.multiple_of(i * R, R), R)
        first = s.n1[rows, :] * s.gain(0) + s.bias(3 * D, 0, D)
        u = first + (s.att[rows, :] + s.bias(4 * D + FF, 0, D))
        c = u - jnp.sum(u, axis=1, keepdims=True) * (1.0 / D)
        r = lax.rsqrt(jnp.sum(c * c, axis=1, keepdims=True) * (1.0 / D) + epsilon)
        n = c * r
        s.out[rows, :] = (n * s.gain(D) + s.bias(5 * D + FF, 0, D)).astype(bf16)
        dy = s.cot[rows, :].astype(f32)
        s.acc_g2[...] += fold(dy * n)
        s.acc_s2[...] += fold(dy)
        e = dy * s.gain(D)
        m1 = jnp.sum(e, axis=1, keepdims=True) * (1.0 / D)
        m2 = jnp.sum(e * n, axis=1, keepdims=True) * (1.0 / D)
        du = r * (e - m1 - n * m2)
        s.dsec[rows, :] = du
        dl = du.astype(bf16)
        s.douter[rows, :] = dl
        s.acc_down[...] += fold(dl.astype(f32))
        return carry
    lax.fori_loop(0, T // R, step, 0)


def stage_ffn_back(s, lo, hi):
    T, D = s.x.shape
    gw, fg = D // GROUPS, FF // GROUPS
    R = 256
    if lo == 0:
        s.acc_up[...] = jnp.zeros_like(s.acc_up)
    def step(i, carry):
        rows = pl.ds(pl.multiple_of(i * R, R), R)
        for pair in range(2):
            outs = []
            for g in (2 * pair, 2 * pair + 1):
                da = dot_nt(s.douter[rows, g * gw:(g + 1) * gw], s.wdown[g])
                di = (da * s.gp[rows, g * fg:(g + 1) * fg]).astype(bf16)
                s.dinner[rows, g * fg:(g + 1) * fg] = di
                s.acc_up[:, g * fg:(g + 1) * fg] += fold(di.astype(f32))
                outs.append(dot_nt(di, s.wup[g]))
            s.att[rows, pair * 2 * gw:(pair + 1) * 2 * gw] = jnp.concatenate(outs, axis=1)
        return carry
    lax.fori_loop(T * lo // (4 * R), T * hi // (4 * R), step, 0)


def stage_down_grad(s, put):
    T, D = s.x.shape
    gw, fg = D // GROUPS, FF // GROUPS
    for g in range(GROUPS):
        put(g, dot_tn(s.active[:, g * fg:(g + 1) * fg], s.douter[:, g * gw:(g + 1) * gw]))


def stage_up_grad(s, put):
    T, D = s.x.shape
    gw, fg = D // GROUPS, FF // GROUPS
    for g in range(GROUPS):
        put(g, dot_tn(s.first_low[:, g * gw:(g + 1) * gw], s.dinner[:, g * fg:(g + 1) * fg]))


def stage_ln1_back(s):
    T, D = s.x.shape
    R = 128
    for a in (s.acc_g1, s.acc_s1, s.acc_out):
        a[...] = jnp.zeros_like(a)
    def step(i, carry):
        rows = pl.ds(pl.multiple_of(i * R, R), R)
        dy = s.dsec[rows, :] + s.att[rows, :]
        n = s.n1[rows, :]
        s.acc_g1[...] += fold(dy * n)
        s.acc_s1[...] += fold(dy)
        e = dy * s.gain(0)
        m1 = jnp.sum(e, axis=1, keepdims=True) * (1.0 / D)
        m2 = jnp.sum(e * n, axis=1, keepdims=True) * (1.0 / D)
        du = s.r1[rows, 0:1] * (e - m1 - n * m2)
        s.dsec[rows, :] = du
        dl = du.astype(bf16)
        s.dattn[rows, :] = dl
        s.acc_out[...] += fold(dl.astype(f32))
        return carry
    lax.fori_loop(0, T // R, step, 0)


def stage_out_grad(s, put):
    put(dot(s.ctxT[...], s.dattn[...]))
    s.dctx[...] = dot_nt(s.dattn[...], s.wout[...]).astype(bf16)


def stage_attn_back(s, lo, hi):
    T, D = s.x.shape
    lane = lax.broadcasted_iota(jnp.int32, (1, 128), 1)
    def pair_step(pr, carry):
        start = pl.multiple_of(pr * 128, 128)
        cols = pl.ds(start, 128)
        q2 = s.q[:, cols]
        v2 = s.v[:, cols]
        dc2 = s.dctx[:, cols]
        kT = s.k[:, cols].T
        prod = (s.ctxT[cols, :].astype(f32)) * (dc2.T.astype(f32))
        dk, dv, dqT = [], [], []
        for h in range(2):
            keep = (lane < 64) if h == 0 else (lane >= 64)
            qm = jnp.where(keep, q2, jnp.zeros_like(q2))
            dcm = jnp.where(keep, dc2, jnp.zeros_like(dc2))
            p = s.pT[2 * pr + h]
            delta = jnp.sum(prod[64 * h:64 * h + 64], axis=0, keepdims=True)
            dp = dot_nt(v2, dcm)
            ds = (p.astype(f32) * (dp - delta)).astype(bf16)
            dv.append(dot(p, dcm))
            dk.append(dot(ds, qm))
            dqT.append(dot(kT[64 * h:64 * h + 64], ds))
        s.dv[:, cols] = (dv[0] + dv[1]).astype(bf16)
        s.dk[:, cols] = (dk[0] + dk[1]).astype(bf16)
        s.dq[:, cols] = (jnp.concatenate(dqT, axis=0) * 0.125).astype(bf16).T
        return carry
    lax.fori_loop(lo, hi, pair_step, 0)


def stage_qkv_grad(s, half, put):
    T, D = s.x.shape
    gw = D // GROUPS
    cols = pl.ds(pl.multiple_of(half * 2 * gw, 128), 2 * gw)
    xh, dq, dk, dv = s.x[:, cols], s.dq[:, cols], s.dk[:, cols], s.dv[:, cols]
    for i in range(2):
        c = slice(i * gw, (i + 1) * gw)
        joined = jnp.concatenate([dq[:, c], dk[:, c], dv[:, c]], axis=1)
        s.joined[2 * half + i] = joined
        put(2 * half + i, i, dot_tn(xh[:, c], joined))


def stage_qkv_grad_one(s, half, i, put):
    T, D = s.x.shape
    gw = D // GROUPS
    cols = pl.ds(pl.multiple_of(half * 2 * gw, 128), 2 * gw)
    xh, dq, dk, dv = (lax.select_n(i == 0, v[:, gw:], v[:, :gw]) for v in (s.x[:, cols], s.dq[:, cols], s.dk[:, cols], s.dv[:, cols]))
    joined = jnp.concatenate([dq, dk, dv], axis=1)
    s.joined[2 * half + i] = joined
    put(2 * half + i, i, dot_tn(xh, joined))


def stage_input_grad(s):
    T, D = s.x.shape
    gw = D // GROUPS
    for pair in range(2):
        cols = slice(pair * 2 * gw, (pair + 1) * 2 * gw)
        outs = [dot_nt(s.joined[g], s.wqkv[g]) for g in (2 * pair, 2 * pair + 1)]
        s.din[:, cols] = s.dsec[:, cols] + jnp.concatenate(outs, axis=1)


MESH = pl.DeviceIdType.MESH
ARRAYS = ("small", "qkv", "out", "up", "down")
NEAR = ("small", "qkv")


class Names:
    pass


class Torus:
    def __init__(self, sizes):
        self.nx, gy = sizes
        self.nc = 2
        assert gy % self.nc == 0
        self.nz = 4 if (gy // self.nc) % 4 == 0 else 1
        self.ny = gy // self.nc // self.nz
        self.count = self.nx * gy
        self.square = self.nx == 2 and self.ny == 2
        self.flat = self.ny * self.nz
        self.near_first = self.nx == 2
        self.quads = self.near_first and self.nz == 4

    def locate(self):
        gy = lax.axis_index("gy")
        self.x = lax.axis_index("gx")
        self.c = gy % self.nc
        self.y = gy // self.nc % self.ny
        self.z = gy // (self.nc * self.ny)

    def device(self, x, y, z, c):
        return (x, (z * self.ny + y) * self.nc + c)

    def sibling(self):
        return self.device(self.x, self.y, self.z, 1 - self.c)

    def place(self, x, y, z, c):
        return ((c * self.nx + x) * self.ny + y) * self.nz + z

    def near_place(self, x, y, z, c):
        return ((c * self.nx + x) * self.nz + z) * self.ny + y

    def place_in(self, x, gy, near):
        place = self.near_place if near else self.place
        return place(x, gy // self.nc % self.ny, gy // (self.nc * self.ny), gy % self.nc)

    def place_of(self, index, near):
        gy_size = self.flat * self.nc
        return self.place_in(index // gy_size, index % gy_size, near)

    def shift(self, o):
        return (self.x + o[0]) % self.nx, (self.y + o[1]) % self.ny

    def turn(self, o):
        return (self.y + o[0]) % self.ny, (self.z + o[1]) % self.nz

    def plane_offsets(self):
        return [(i, j) for i in range(self.nx) for j in range(self.ny) if i or j]

    def flat_offsets(self):
        return [(i, j) for j in range(self.nz) for i in range(self.ny) if i or j]

    def peers(self):
        found = [self.device(self.x, y, z, self.c) for y, z in (self.turn(o) for o in self.flat_offsets())]
        for o in self.plane_offsets():
            if o[0] == 0 or (self.square and o == (1, 1)):
                continue
            px, py = self.shift(o)
            found.append(self.device(px, py, self.z, self.c))
        return found + [self.sibling()]


def remote(src, dst, send, recv, device):
    return pltpu.make_async_remote_copy(
        src_ref=src, dst_ref=dst, send_sem=send, recv_sem=recv, device_id=device, device_id_type=MESH
    )


class NearGather:
    def __init__(self, t, own, buf, sems):
        self.t, self.own, self.buf = t, own, buf
        self.local, self.s1, self.r1, self.s2, self.r2, self.s3, self.r3 = sems

    def chunk(self, x, c):
        return self.buf.at[pl.ds(self.t.near_place(x, 0, 0, c), self.t.flat)]

    def local_copy(self):
        t = self.t
        return pltpu.make_async_copy(self.own, self.buf.at[t.near_place(t.x, t.y, t.z, t.c)], self.local.at[0])

    def near_copies(self):
        t = self.t
        mine = self.buf.at[t.near_place(t.x, t.y, t.z, t.c)]
        found = []
        for k, o in enumerate(t.flat_offsets()):
            py, pz = t.turn(o)
            found.append(remote(self.own, mine, self.s1.at[k], self.r1.at[k], t.device(t.x, py, pz, t.c)))
        return found

    def far_copy(self, d):
        t = self.t
        part = self.chunk(t.x, t.c)
        return remote(part, part, self.s2.at[d], self.r2.at[d], t.device((t.x + d) % t.nx, t.y, t.z, t.c))

    def core_copy(self, d):
        t = self.t
        part = self.chunk((t.x + t.nx - d) % t.nx, t.c)
        return remote(part, part, self.s3.at[d], self.r3.at[d], t.sibling())

    def begin(self):
        self.local_copy().start()
        for c in self.near_copies():
            c.start()

    def spread(self):
        for c in self.near_copies():
            c.wait_recv()
        self.local_copy().wait()
        self.core_copy(0).start()
        for d in range(1, self.t.nx):
            self.far_copy(d).start()

    def near_done(self):
        self.core_copy(0).wait_recv()

    def share(self):
        for d in range(1, self.t.nx):
            self.far_copy(d).wait_recv()
            self.core_copy(d).start()

    def far_done(self):
        for d in range(1, self.t.nx):
            self.core_copy(d).wait_recv()

    def close(self):
        for c in self.near_copies():
            c.wait_send()
        for d in range(self.t.nx):
            self.core_copy(d).wait_send()
            if d:
                self.far_copy(d).wait_send()


class NearScatter:
    def __init__(self, t, buf, ra, rb, rc, sems):
        self.t, self.buf, self.ra, self.rb, self.rc = t, buf, ra, rb, rc
        self.s1, self.r1, self.s2, self.r2, self.s3, self.r3 = sems

    halves = False

    def turn(self, o):
        t = self.t
        if not self.halves:
            return t.turn(o)
        return (t.y + o[0]) % 2, (t.z // 2 + o[1]) % 2 * 2 + (t.z + o[2]) % 2

    def offsets(self):
        if not self.halves:
            return [self.t.flat_offsets()]
        return [[(i, a, b) for i in range(2) for b in range(2) if i or a or b] for a in range(2)]

    def far_core_copy(self, d):
        t = self.t
        part = self.buf.at[pl.ds(t.near_place((t.x + d) % t.nx, 0, 0, 1 - t.c), t.flat)]
        return remote(part, self.ra.at[d], self.s1.at[d], self.r1.at[d], t.sibling())

    def far_copy(self, d):
        t = self.t
        return remote(self.ra.at[d], self.rb.at[d], self.s2.at[d], self.r2.at[d],
                      t.device((t.x + d) % t.nx, t.y, t.z, t.c))

    def span(self, part):
        t = self.t
        if not self.halves:
            return 0, t.flat
        return (t.z // 2 + part) % 2 * 2 * t.ny, 2 * t.ny

    def core_copy(self, part):
        t = self.t
        start, n = self.span(part)
        k = part * t.nx
        return remote(self.buf.at[pl.ds(t.near_place(t.x, 0, 0, 1 - t.c) + start, n)], self.ra.at[0, pl.ds(start, n)],
                      self.s1.at[k], self.r1.at[k], t.sibling())

    def flat_copies(self, part):
        t = self.t
        lists = self.offsets()
        first = sum(len(l) for l in lists[:part])
        found = []
        for k, o in enumerate(lists[part]):
            py, pz = self.turn(o)
            found.append(remote(self.ra.at[0, pz * t.ny + py], self.rc.at[first + k], self.s3.at[first + k],
                                self.r3.at[first + k], t.device(t.x, py, pz, t.c)))
        return found

    def begin_far(self):
        for d in range(1, self.t.nx):
            self.far_core_copy(d).start()

    def far(self):
        t = self.t
        for d in range(1, t.nx):
            self.far_core_copy(d).wait_recv()
            part = self.buf[pl.ds(t.near_place((t.x + d) % t.nx, 0, 0, t.c), t.flat)]
            self.ra[d] = (part.astype(f32) + self.ra[d].astype(f32)).astype(self.ra.dtype)
            self.far_copy(d).start()

    def begin_near(self, part):
        self.core_copy(part).start()

    def near(self, part):
        t = self.t
        start, n = self.span(part)
        self.core_copy(part).wait_recv()
        if part == len(self.offsets()) - 1:
            for d in range(1, t.nx):
                self.far_copy(d).wait_recv()
        own = self.buf[pl.ds(t.near_place(t.x, 0, 0, t.c) + start, n)]
        total = own.astype(f32) + self.ra[0, pl.ds(start, n)].astype(f32)
        for d in range(1, t.nx):
            total = total + self.rb[d, pl.ds(start, n)].astype(f32)
        self.ra[0, pl.ds(start, n)] = total.astype(self.ra.dtype)
        for c in self.flat_copies(part):
            c.start()

    def total(self):
        t = self.t
        total = self.ra[0, t.z * t.ny + t.y].astype(f32)
        k = 0
        for part in range(len(self.offsets())):
            for c in self.flat_copies(part):
                c.wait_recv()
                total = total + self.rc[k].astype(f32)
                k += 1
        return total

    def close(self):
        t = self.t
        for part in range(len(self.offsets())):
            self.core_copy(part).wait_send()
            for c in self.flat_copies(part):
                c.wait_send()
        for d in range(1, t.nx):
            self.far_core_copy(d).wait_send()
            self.far_copy(d).wait_send()


class Planes:
    def route(self):
        t = self.t
        if t.square:
            self.offsets = [(t.c, 1 - t.c), (1 - t.c, t.c)]
        else:
            self.offsets = t.plane_offsets()

    def slot(self, o):
        return o[0] * self.t.ny + o[1]

    def to(self, o):
        px, py = self.t.shift(o)
        return self.t.device(px, py, self.t.z, self.t.c)


class Gather(Planes):
    def __init__(self, t, own, buf, sems):
        self.t, self.own, self.buf = t, own, buf
        self.local, self.s1, self.r1, self.s2, self.r2, self.s3, self.r3 = sems
        self.route()

    def chunk(self, x, y):
        return self.buf.at[pl.ds(self.t.place(x, y, 0, self.t.c), self.t.nz)]

    def local_copy(self):
        t = self.t
        return pltpu.make_async_copy(self.own, self.buf.at[t.place(t.x, t.y, t.z, t.c)], self.local.at[0])

    def line_copies(self):
        t = self.t
        mine = self.buf.at[t.place(t.x, t.y, t.z, t.c)]
        return [
            remote(self.own, mine, self.s1.at[d], self.r1.at[d], t.device(t.x, t.y, (t.z + d) % t.nz, t.c))
            for d in range(1, t.nz)
        ]

    def plane_copy(self, k):
        part = self.chunk(self.t.x, self.t.y)
        return remote(part, part, self.s2.at[k], self.r2.at[k], self.to(self.offsets[k]))

    def relay_copy(self):
        part = self.chunk(*self.t.shift(self.offsets[0]))
        return remote(part, part, self.s2.at[2], self.r2.at[2], self.to(self.offsets[1]))

    def core_copy(self, o):
        t = self.t
        part = self.chunk((t.x + t.nx - o[0]) % t.nx, (t.y + t.ny - o[1]) % t.ny)
        k = self.slot(o)
        return remote(part, part, self.s3.at[k], self.r3.at[k], t.sibling())

    def begin(self):
        self.local_copy().start()
        for c in self.line_copies():
            c.start()

    def spread(self):
        for c in self.line_copies():
            c.wait_recv()
        self.local_copy().wait()
        for k in range(len(self.offsets)):
            self.plane_copy(k).start()
        self.core_copy((0, 0)).start()

    def share(self):
        for k, o in enumerate(self.offsets):
            self.plane_copy(k).wait_recv()
            if self.t.square and k == 0:
                self.relay_copy().start()
            self.core_copy(o).start()

    def share_last(self):
        if self.t.square:
            self.relay_copy().wait_recv()
            self.core_copy((1, 1)).start()

    def done(self):
        for o in [(0, 0)] + self.t.plane_offsets():
            self.core_copy(o).wait_recv()

    def close(self):
        for c in self.line_copies():
            c.wait_send()
        for k in range(len(self.offsets)):
            self.plane_copy(k).wait_send()
        if self.t.square:
            self.relay_copy().wait_send()
        for o in [(0, 0)] + self.t.plane_offsets():
            self.core_copy(o).wait_send()


class Scatter(Planes):
    def __init__(self, t, buf, ra, rb, rc, sems):
        self.t, self.buf, self.ra, self.rb, self.rc = t, buf, ra, rb, rc
        self.s1, self.r1, self.s2, self.r2, self.s3, self.r3 = sems
        self.route()

    def core_copy(self, o):
        t = self.t
        px, py = t.shift(o)
        part = self.buf.at[pl.ds(t.place(px, py, 0, 1 - t.c), t.nz)]
        k = self.slot(o)
        return remote(part, self.ra.at[k], self.s1.at[k], self.r1.at[k], t.sibling())

    def plane_copy(self, k, o, to):
        return remote(self.ra.at[self.slot(o)], self.rb.at[k], self.s2.at[k], self.r2.at[k], self.to(to))

    def line_copy(self, d):
        t = self.t
        to = (t.z + d) % t.nz
        return remote(self.ra.at[0, to], self.rc.at[d], self.s3.at[d], self.r3.at[d], t.device(t.x, t.y, to, t.c))

    def hops(self):
        if self.t.square:
            a, b = self.offsets
            return [(0, (1, 1), b), (1, b, b), (2, a, a)]
        return [(k, o, o) for k, o in enumerate(self.offsets)]

    def chip_sum(self, o):
        t = self.t
        px, py = t.shift(o)
        part = self.buf[pl.ds(t.place(px, py, 0, t.c), t.nz)]
        return part.astype(f32) + self.ra[self.slot(o)].astype(f32)

    def begin(self):
        for o in self.t.plane_offsets() + [(0, 0)]:
            self.core_copy(o).start()

    def planes(self):
        for o in self.t.plane_offsets() + [(0, 0)]:
            self.core_copy(o).wait_recv()
        for k, o, to in self.hops()[:2] if self.t.square else self.hops():
            self.ra[self.slot(o)] = self.chip_sum(o).astype(self.ra.dtype)
            self.plane_copy(k, o, to).start()

    def planes_last(self):
        if self.t.square:
            hops = self.hops()
            self.plane_copy(*hops[0]).wait_recv()
            k, o, to = hops[2]
            self.ra[self.slot(o)] = (self.chip_sum(o) + self.rb[0].astype(f32)).astype(self.ra.dtype)
            self.plane_copy(k, o, to).start()

    def line(self):
        t = self.t
        total = self.chip_sum((0, 0))
        for k, o, to in self.hops()[1:] if t.square else self.hops():
            self.plane_copy(k, o, to).wait_recv()
            total = total + self.rb[k].astype(f32)
        self.ra[0] = total.astype(self.ra.dtype)
        for d in range(1, t.nz):
            self.line_copy(d).start()

    def total(self):
        t = self.t
        total = self.ra[0, t.z].astype(f32)
        for d in range(1, t.nz):
            self.line_copy(d).wait_recv()
            total = total + self.rc[d].astype(f32)
        return total

    def close(self):
        for d in range(1, self.t.nz):
            self.line_copy(d).wait_send()
        for hop in self.hops():
            self.plane_copy(*hop).wait_send()
        for o in self.t.plane_offsets() + [(0, 0)]:
            self.core_copy(o).wait_send()


def swap_halves(a, b):
    lane = lax.broadcasted_iota(jnp.int32, a.shape, 1)
    return jnp.where(lane < 64, pltpu.roll(a, 64, 1), pltpu.roll(b, 64, 1))


def lines_to_rows(lines, spare, rows, width):
    if width % 128 == 0:
        m = width // 128
        return jnp.concatenate([lines[pl.ds(j, rows, stride=m), :] for j in range(m)], axis=1).astype(bf16)
    m = width // 64
    q, half = m // 2, rows // 2
    a = [lines[pl.ds(j, half, stride=m), :] for j in range(m)]
    for j in range(q + 1):
        spare[j, pl.ds(0, half, stride=2), :] = a[j]
        spare[j, pl.ds(1, half, stride=2), :] = swap_halves(a[q + j], a[q + j + 1] if j < q else a[q + j])
    return jnp.concatenate([spare[j] for j in range(q)] + [spare[q][:, 0:64]], axis=1).astype(bf16)


def rows_to_lines(value, lines, spare):
    rows, width = value.shape
    if width % 128 == 0:
        m = width // 128
        for j in range(m):
            lines[pl.ds(j, rows, stride=m), :] = value[:, 128 * j:128 * j + 128]
        return
    m = width // 64
    q, half = m // 2, rows // 2
    for j in range(q):
        spare[j] = value[:, 128 * j:128 * j + 128]
    spare[q, :, 0:64] = value[:, 128 * q:width]
    even = [spare[j, pl.ds(0, half, stride=2), :] for j in range(q + 1)]
    odd = [spare[j, pl.ds(1, half, stride=2), :] for j in range(q + 1)]
    lane = lax.broadcasted_iota(jnp.int32, even[0].shape, 1)
    for j in range(q):
        lines[pl.ds(j, half, stride=m), :] = even[j]
        lines[pl.ds(q + 1 + j, half, stride=m), :] = swap_halves(odd[j], odd[j + 1])
    lines[pl.ds(q, half, stride=m), :] = jnp.where(lane < 64, even[q], pltpu.roll(odd[0], 64, 1))


def group_places(t, g, half, i, near):
    per = t.count // GROUPS
    if t.nx == 2:
        return [t.place_in(half, i * per + j, near) for j in range(per)]
    return [t.place_of(g * per + j, near) for j in range(per)]


def group_weight(s, t, name, places):
    buf = s.held[name]
    rows, width = s.group_shape[name]
    if s.lined:
        n = buf.shape[1]
        for j, p in enumerate(places):
            s.lines[n * j:n * j + n, :] = buf[p].astype(f32)
        return lines_to_rows(s.lines, s.spare[width], rows, width)
    return jnp.concatenate([buf[p].astype(f32) for p in places], axis=0).astype(bf16)


def assemble_small(s, t):
    nb, ng = s.small_sizes
    buf = s.held["small"]
    for d in range(t.count):
        p = t.place_of(d, True)
        s.bias_v[0:1, nb * d:nb * d + nb] = buf[p, 0:1, 0:nb]
        s.gain_v[0:1, ng * d:ng * d + ng] = buf[p, 0:1, nb:nb + ng]


def assemble_qkv(s, t, half):
    for i in range(2):
        g = 2 * half + i
        s.wqkv[g] = group_weight(s, t, "qkv", group_places(t, g, half, i, True))


def assemble(s, t, name):
    for g in range(GROUPS):
        value = group_weight(s, t, name, group_places(t, g, g // 2, g % 2, False))
        if name == "out":
            gw = s.wout.shape[0] // GROUPS
            s.wout[g * gw:(g + 1) * gw, :] = value
        elif name == "up":
            s.wup[g] = value
        else:
            s.wdown[g] = value


def lay_out(s, t, name, places, value):
    buf = s.held[name]
    if s.lined:
        n = buf.shape[1]
        rows_to_lines(value, s.lines, s.spare[value.shape[1]] if value.shape[1] % 128 else None)
        for j, p in enumerate(places):
            buf[p] = s.lines[n * j:n * j + n, :].astype(bf16)
        return
    rows = value.shape[0] // len(places)
    for j, p in enumerate(places):
        buf[p] = value[rows * j:rows * j + rows].astype(bf16)


def lay_out_small(s, t):
    T, D = s.x.shape
    nb, ng = s.small_sizes
    def rs(v):
        return jnp.sum(v, axis=0, keepdims=True)
    s.bias_v[:, 0:D] = rs(s.dq[...].astype(f32))
    s.bias_v[:, D:2 * D] = rs(s.dv[...].astype(f32))
    s.bias_v[:, 2 * D:3 * D] = rs(s.acc_out[...])
    s.bias_v[:, 3 * D:4 * D] = rs(s.acc_s1[...])
    s.bias_v[:, 4 * D:4 * D + FF] = rs(s.acc_up[...])
    s.bias_v[:, 4 * D + FF:5 * D + FF] = rs(s.acc_down[...])
    s.bias_v[:, 5 * D + FF:] = rs(s.acc_s2[...])
    s.gain_v[:, 0:D] = rs(s.acc_g1[...])
    s.gain_v[:, D:] = rs(s.acc_g2[...])
    buf = s.held["small"]
    for d in range(t.count):
        p = t.place_of(d, True)
        buf[p, 0:1, 0:nb] = s.bias_v[0:1, nb * d:nb * d + nb]
        buf[p, 0:1, nb:nb + ng] = s.gain_v[0:1, ng * d:ng * d + ng]


def layer_kernel(names, t, small_sizes, group_shape, lined, *refs):
    s = Names()
    for n, r in zip(names, refs, strict=True):
        setattr(s, n, r)
    D = s.x.shape[1]
    nb, ng = small_sizes
    s.small_sizes, s.group_shape, s.lined = small_sizes, group_shape, lined
    s.bias = lambda base, off, w: s.bias_v[0:1, base + off:base + off + w]
    s.gain = lambda base: s.gain_v[0:1, base:base + D]
    s.held = {n: getattr(s, "held_" + n) for n in ARRAYS}
    if lined:
        s.spare = {D // GROUPS * 3: s.spare_wide, D // GROUPS: s.spare_tall, D: None}
    t.locate()
    s.in_small[0:1, 0:nb] = s.in_bias[...].astype(f32).reshape(1, nb)
    s.in_small[0:1, nb:nb + ng] = s.in_gain[...].astype(f32).reshape(1, ng)

    barrier = pltpu.get_barrier_semaphore()
    peers = t.peers()
    for peer in peers:
        pl.semaphore_signal(barrier, inc=1, device_id=peer, device_id_type=MESH)
    pl.semaphore_wait(barrier, len(peers))

    gather, scatter = {}, {}
    for i, n in enumerate(ARRAYS):
        make = (NearGather, NearScatter) if n in NEAR else (Gather, Scatter)
        gather[n] = make[0](t, getattr(s, "in_" + n), s.held[n],
                            [getattr(s, "g_" + k).at[i] for k in ("local", "s1", "r1", "s2", "r2", "s3", "r3")])
        scatter[n] = make[1](t, s.held[n], *[getattr(s, k + "_" + n) for k in ("ra", "rb", "rc")],
                             [getattr(s, "h_" + k).at[i] for k in ("s1", "r1", "s2", "r2", "s3", "r3")])
    scatter["qkv"].halves = t.quads
    near_first = t.near_first
    half = t.x if near_first else 0
    rest = 1 - half

    take_x = pltpu.make_async_copy(s.x_in, s.x, s.moves.at[0])
    take_cot = pltpu.make_async_copy(s.cot_in, s.cot, s.moves.at[1])
    give_out = pltpu.make_async_copy(s.out, s.out_to, s.moves.at[2])
    give_din = pltpu.make_async_copy(s.din, s.din_to, s.moves.at[3])

    gather["small"].begin()
    gather["qkv"].begin()
    take_x.start()
    take_cot.start()
    stage_mask(s)
    gather["small"].spread()
    gather["small"].share()
    gather["out"].begin()
    gather["qkv"].spread()
    gather["up"].begin()
    gather["down"].begin()
    gather["small"].near_done()
    gather["small"].far_done()
    assemble_small(s, t)
    take_x.wait()
    gather["qkv"].near_done()
    if not near_first:
        gather["qkv"].share()
        gather["qkv"].far_done()
    assemble_qkv(s, t, half)
    stage_qkv(s, half)
    stage_attn_fwd(s, 3 * half, 3 * half + 1)
    gather["out"].spread()
    stage_attn_fwd(s, 3 * half + 1, 3 * half + 2)
    if near_first:
        gather["qkv"].share()
    stage_attn_fwd(s, 3 * half + 2, 3 * half + 3)
    gather["up"].spread()
    gather["out"].share()
    if near_first:
        gather["qkv"].far_done()
    assemble_qkv(s, t, rest)
    stage_qkv(s, rest)
    gather["down"].spread()
    stage_attn_fwd(s, 3 * rest, 3 * rest + 1)
    gather["out"].share_last()
    gather["up"].share()
    stage_attn_fwd(s, 3 * rest + 1, 3 * rest + 2)
    stage_attn_fwd(s, 3 * rest + 2, 3 * rest + 3)
    gather["out"].done()
    assemble(s, t, "out")
    gather["down"].share()
    stage_ln1(s)
    gather["up"].share_last()
    gather["down"].share_last()
    gather["up"].done()
    assemble(s, t, "up")
    gather["down"].done()
    assemble(s, t, "down")
    for n in ARRAYS:
        gather[n].close()
    stage_ffn(s)
    take_cot.wait()
    stage_ln2(s)
    give_out.start()

    def put(name):
        return lambda g, v: lay_out(s, t, name, group_places(t, g, g // 2, g % 2, False), v)

    stage_down_grad(s, put("down"))
    scatter["down"].begin()
    stage_ffn_back(s, 0, 2)
    scatter["down"].planes()
    stage_ffn_back(s, 2, 4)
    stage_up_grad(s, put("up"))
    scatter["up"].begin()
    stage_ln1_back(s)
    scatter["up"].planes()
    def put_out(v):
        gw = D // GROUPS
        for g in range(GROUPS):
            put("out")(g, v[g * gw:(g + 1) * gw])
    stage_out_grad(s, put_out)
    scatter["out"].begin()
    scatter["down"].planes_last()
    stage_attn_back(s, 3 * rest, 3 * rest + 1)
    scatter["out"].planes()
    stage_attn_back(s, 3 * rest + 1, 3 * rest + 2)
    scatter["up"].planes_last()
    stage_attn_back(s, 3 * rest + 2, 3 * rest + 3)
    scatter["down"].line()
    put_qkv = lambda h: lambda g, i, v: lay_out(s, t, "qkv", group_places(t, g, h, i, True), v)
    stage_qkv_grad(s, rest, put_qkv(rest))
    if near_first:
        scatter["qkv"].begin_far()
    zh = t.z // 2 if t.quads else 0
    first = 3 * half + (2 - 2 * zh if t.quads else 0)
    last = 3 * half + (2 * zh if t.quads else 2)
    stage_attn_back(s, first, first + 1)
    if near_first:
        scatter["qkv"].far()
    scatter["out"].planes_last()
    stage_attn_back(s, 3 * half + 1, 3 * half + 2)
    if t.quads:
        stage_qkv_grad_one(s, half, 1 - zh, put_qkv(half))
        scatter["qkv"].begin_near(1)
    scatter["up"].line()
    s.grad_down[...] = scatter["down"].total()
    stage_attn_back(s, last, last + 1)
    if t.quads:
        scatter["qkv"].near(1)
    lay_out_small(s, t)
    scatter["small"].begin_far()
    scatter["small"].begin_near(0)
    scatter["out"].line()
    scatter["small"].far()
    if t.quads:
        stage_qkv_grad_one(s, half, zh, put_qkv(half))
    else:
        stage_qkv_grad(s, half, put_qkv(half))
    if not near_first:
        scatter["qkv"].begin_far()
        scatter["qkv"].far()
    scatter["qkv"].begin_near(0)
    stage_input_grad(s)
    give_din.start()
    scatter["qkv"].near(0)
    scatter["small"].near(0)
    s.grad_up[...] = scatter["up"].total()
    s.grad_out[...] = scatter["out"].total()
    s.grad_qkv[...] = scatter["qkv"].total()
    small = scatter["small"].total()
    s.grad_bias[...] = small[:, 0:nb]
    s.grad_gain[...] = small[:, nb:nb + ng]
    give_out.wait()
    give_din.wait()
    for n in ARRAYS:
        scatter[n].close()


def hand_on(count, *refs):
    held, sems = refs[2 * count:3 * count], refs[3 * count]
    taken = [pltpu.make_async_copy(refs[i], held[i], sems.at[0, i]) for i in range(count)]
    given = [pltpu.make_async_copy(held[i], refs[count + i], sems.at[1, i]) for i in range(count)]
    for c in taken:
        c.start()
    for i in range(count):
        taken[i].wait()
        given[i].start()
    for c in given:
        c.wait()


def body(sizes, hidden_in, segment_ids, positions, token_mask, cotangent, qkv_weight, out_weight, up_weight, down_weight, biases, gains):
    rows, T, D = hidden_in.shape
    assert rows == 1
    gw, fg = D // GROUPS, FF // GROUPS
    t = Torus(sizes)
    nb, ng = biases.shape[0], gains.shape[0]
    depth = D // t.count
    group_shape = {"qkv": (gw, 3 * gw), "out": (gw, D), "up": (gw, fg), "down": (fg, gw)}
    lined = all(v.shape[0] % 512 == 0 for v in (qkv_weight, out_weight, up_weight, down_weight))
    blocks = {"small": ((1, nb + ng), f32)}
    for n, flat in zip(ARRAYS[1:], (qkv_weight, out_weight, up_weight, down_weight)):
        size = flat.shape[0]
        blocks[n] = ((size // 128, 128) if lined else (size // group_shape[n][1], group_shape[n][1]), bf16)
    inputs = {
        "x_in": hidden_in[0], "seg": segment_ids, "pos": positions, "tok": token_mask, "cot_in": cotangent[0],
        "in_bias": biases, "in_gain": gains,
        "in_qkv": qkv_weight.reshape(blocks["qkv"][0]),
        "in_out": out_weight.reshape(blocks["out"][0]),
        "in_up": up_weight.reshape(blocks["up"][0]),
        "in_down": down_weight.reshape(blocks["down"][0]),
    }
    outputs = {"out_to": ((T, D), bf16), "din_to": ((T, D), f32)}
    for n in ARRAYS[1:]:
        outputs["grad_" + n] = (blocks[n][0], f32)
    outputs["grad_bias"] = ((1, nb), f32)
    outputs["grad_gain"] = ((1, ng), f32)
    scratch = dict(
        x=((T, D), bf16), cot=((T, D), bf16), out=((T, D), bf16), din=((T, D), f32),
        mask=((T, T), f32), q=((T, D), bf16), k=((T, D), bf16), v=((T, D), bf16), pT=((HEADS, T, T), bf16),
        ctx=((T, D), bf16), ctxT=((D, T), bf16), att=((T, D), f32), n1=((T, D), f32), r1=((T, 128), f32),
        first_low=((T, D), bf16), active=((T, FF), bf16), gp=((T, FF), f32), dsec=((T, D), f32),
        douter=((T, D), bf16), dinner=((T, FF), bf16), dattn=((T, D), bf16), dctx=((T, D), bf16),
        dq=((T, D), bf16), dk=((T, D), bf16), dv=((T, D), bf16), joined=((GROUPS, T, 3 * gw), bf16),
        acc_g2=((8, D), f32), acc_s2=((8, D), f32), acc_down=((8, D), f32), acc_up=((8, FF), f32),
        acc_g1=((8, D), f32), acc_s1=((8, D), f32), acc_out=((8, D), f32),
        in_small=((1, nb + ng), f32), bias_v=((1, nb * t.count), f32), gain_v=((1, ng * t.count), f32),
        wqkv=((GROUPS, gw, 3 * gw), bf16), wout=((D, D), bf16), wup=((GROUPS, gw, fg), bf16),
        wdown=((GROUPS, fg, gw), bf16),
    )
    if lined:
        scratch["lines"] = ((fg * gw // 128, 128), f32)
        scratch["spare_wide"] = ((3 * gw // 128 + 1, gw, 128), f32)
        scratch["spare_tall"] = ((gw // 128 + 1, fg, 128), f32)
    planes = t.nx * t.ny
    for n in ARRAYS:
        shape, kind = blocks[n]
        scratch["held_" + n] = ((t.count,) + shape, kind)
        near = n in NEAR
        scratch["ra_" + n] = ((t.nx, t.flat) if near else (planes, t.nz)) + shape, kind
        scratch["rb_" + n] = ((t.nx, t.flat) if near else (planes - 1, t.nz)) + shape, kind
        scratch["rc_" + n] = ((t.flat - 1,) if near else (t.nz,)) + shape, kind
    shapes = [pltpu.VMEM(*scratch[n]) for n in scratch]
    most = max(planes, t.flat)
    sems = ["g_local", "g_s1", "g_r1", "g_s2", "g_r2", "g_s3", "g_r3", "h_s1", "h_r1", "h_s2", "h_r2", "h_s3", "h_r3"]
    shapes += [pltpu.SemaphoreType.DMA((len(ARRAYS), most)) for n in sems]
    shapes.append(pltpu.SemaphoreType.DMA((4,)))
    names = list(inputs) + list(outputs) + list(scratch) + list(sems) + ["moves"]
    vm = pl.BlockSpec(memory_space=pltpu.VMEM)
    anywhere = pl.BlockSpec(memory_space=pl.ANY)
    found = pl.pallas_call(
        lambda *refs: layer_kernel(names, t, (nb, ng), group_shape, lined, *refs),
        out_shape=[jax.ShapeDtypeStruct(*outputs[n]) for n in outputs],
        in_specs=[anywhere if n in ("x_in", "cot_in") else vm for n in inputs],
        out_specs=[anywhere if n in ("out_to", "din_to") else vm for n in outputs],
        scratch_shapes=shapes,
        compiler_params=pltpu.CompilerParams(
            collective_id=0, has_side_effects=True, vmem_limit_bytes=67043328
        ),
        name="layer",
    )(*inputs.values())
    count = len(outputs)
    found = pl.pallas_call(
        lambda *refs: hand_on(count, *refs),
        out_shape=[jax.ShapeDtypeStruct(*outputs[n]) for n in outputs],
        in_specs=[anywhere] * count,
        out_specs=[anywhere] * count,
        scratch_shapes=[pltpu.VMEM(*outputs[n]) for n in outputs] + [pltpu.SemaphoreType.DMA((2, count))],
        name="hand_on",
    )(*found)
    o = dict(zip(outputs, found))
    return (
        o["out_to"][None], o["din_to"][None], o["grad_qkv"].reshape(-1), o["grad_out"].reshape(-1), o["grad_up"].reshape(-1),
        o["grad_down"].reshape(-1), o["grad_bias"].reshape(-1), o["grad_gain"].reshape(-1),
    )


def solution(mesh):
    whole = P(("gx", "gy"))
    rows2 = P(("gx", "gy"), None)
    rows3 = P(("gx", "gy"), None, None)
    sizes = (mesh.shape["gx"], mesh.shape["gy"])
    return jax.shard_map(
        lambda *args: body(sizes, *args),
        mesh=mesh,
        in_specs=(rows3, rows2, rows2, rows2, rows3) + (whole,) * 6,
        out_specs=(rows3, rows3) + (whole,) * 6,
        check_vma=False,
    )
```
